256 devices in a mesh: prow: 8 (over x, core), pcol: 32 (over z, y).
Axes of the slice: x: 4, y: 4, z: 8, core: 2. Of those that a mesh axis runs over, the one named last changes fastest.
Arguments:
- matrix: bfloat16 [5, 4096, 2, 16384], P(None, 'prow', None, 'pcol'), may hold values from -6 to 6
- pivots: int32 [2, 512], replicated, may hold values from 0 to 20479, as said below
- lower_inverse: bfloat16 [2, 512, 512], replicated, as said below
- upper_inverse: bfloat16 [2, 512, 512], replicated, as said below
Outputs:
- factored: bfloat16 [5, 4096, 2, 16384], P(None, 'prow', None, 'pcol')
The draws below stay inside these ranges and needn't reach their ends.
Inputs may be any that keep to these rules, and one draw needn't show every extreme that they name: `pivots`: for panel k, entry i is either k * 512 + i (the row stays) or a row from (k + 1) * 512 on; the entries of one panel are distinct; entry 511 of each panel is 20479, and entry 0 of panel 0 is 0. Each lower_inverse[k] is unit lower triangular. Each upper_inverse[k] is upper triangular with a positive diagonal.
All inputs are finite; a program needn't handle non-finite values.
Results may differ from the reference program's by a relative error of at most 0.0084.
Values may be sent and summed in bfloat16 or wider, within the bound.
A program may use at most 128 MiB of HBM per device.

```python
import math
import jax
import jax.numpy as jnp
from jax import lax

NB = 512
CB_DEV = 2
RB_DEV = 5
STEPS = 2
RSPAN = 4096
CSPAN = 16384
ROWS = 20480
ORDER = 32768


def draw_pivots(key, part):
    picked_rows = []
    for panel_step in range(STEPS):
        panel_key = jax.random.fold_in(key, panel_step)
        begin_row = (panel_step + 1) * NB
        shuffled = jax.random.permutation(jax.random.fold_in(panel_key, 1), ROWS - begin_row)[:NB] + begin_row
        last_place = jnp.argmax(shuffled == ROWS - 1)
        shuffled = shuffled.at[last_place].set(shuffled[NB - 1]).at[NB - 1].set(ROWS - 1)
        staying = jax.random.randint(jax.random.fold_in(panel_key, 2), (NB,), 0, 4) == 0
        if panel_step == 0:
            staying = staying.at[0].set(True)
        staying = staying.at[NB - 1].set(False)
        own_rows = panel_step * NB + jnp.arange(NB)
        picked_rows.append(jnp.where(staying, own_rows, shuffled))
    return jnp.stack(picked_rows).astype(jnp.int32)


def draw_lower_inverse(key, part):
    noise = jax.random.normal(key, (STEPS, NB, NB), jnp.float32)
    strict = jnp.tril(noise * (0.5 / math.sqrt(NB)), -1)
    return (strict + jnp.eye(NB, dtype=jnp.float32)).astype(jnp.bfloat16)


def draw_upper_inverse(key, part):
    noise_key = jax.random.fold_in(key, 11)
    scale_key = jax.random.fold_in(key, 12)
    noise = jax.random.normal(noise_key, (STEPS, NB, NB), jnp.float32)
    diagonal = jnp.exp(jax.random.uniform(scale_key, (STEPS, NB), jnp.float32, math.log(0.5), math.log(2.0)))
    strict = jnp.triu(noise * (0.5 / NB), 1)
    full = strict + (diagonal / math.sqrt(NB))[:, :, None] * jnp.eye(NB, dtype=jnp.float32)
    return full.astype(jnp.bfloat16)


def shard_levels(rng, shape, split, low, top_value):
    def one(dim, blocks):
        draws = jax.random.uniform(jax.random.fold_in(jax.random.fold_in(rng, 6), dim), (blocks,), jnp.float32, low / len(split), top_value / len(split))
        return jnp.repeat(jnp.exp(draws), shape[dim] // blocks).reshape((-1,) + (1,) * (len(shape) - dim - 1))

    factor_of = one(*split[0])
    for cut in split[1:]:
        factor_of = factor_of * one(*cut)
    return factor_of


def gaussian(stream_key, extent, scale, bound, shards=(), held_as=jnp.bfloat16):
    level = shard_levels(stream_key, extent, shards, -0.22, 0.18) if shards else 1.0
    entries = jax.random.normal(stream_key, extent, jnp.float32) * scale * level
    return jnp.minimum(jnp.maximum(entries, -bound), bound).astype(held_as)


def setup_inputs(seed: int = 0) -> dict:
    streams_of = jax.random.split(jax.random.key(seed), 5)
    return {
        "matrix": gaussian(streams_of[0], (RB_DEV, RSPAN, CB_DEV, CSPAN), 1.0, 6.0, ((1, 8), (3, 32))),
        "pivots": draw_pivots(jax.random.fold_in(streams_of[4], 71), 0),
        "lower_inverse": draw_lower_inverse(jax.random.fold_in(streams_of[4], 71), 0),
        "upper_inverse": draw_upper_inverse(jax.random.fold_in(streams_of[4], 71), 0),
    }


def reference(matrix, pivots, lower_inverse, upper_inverse):
    dense = matrix.reshape(ROWS, ORDER)
    for panel_step in range(STEPS):
        top_start = panel_step * NB
        next_start = top_start + NB
        top_index = top_start + jnp.arange(NB, dtype=jnp.int32)
        pivot_index = pivots[panel_step]
        top_values = dense[top_index]
        pivot_values = dense[pivot_index]
        dense = dense.at[pivot_index].set(top_values).at[top_index].set(pivot_values)
        factor = jnp.dot(dense[next_start:, top_start:next_start], upper_inverse[panel_step],
                         preferred_element_type=jnp.float32).astype(jnp.bfloat16)
        top_product = jnp.dot(lower_inverse[panel_step], dense[top_start:next_start, next_start:],
                              preferred_element_type=jnp.float32).astype(jnp.bfloat16)
        dense = dense.at[next_start:, top_start:next_start].set(factor)
        dense = dense.at[top_start:next_start, next_start:].set(top_product)
        upper_wide = top_product.astype(jnp.float32)

        def update_block(block_index, current):
            row_begin = (block_index * NB).astype(jnp.int32)
            row_slab = lax.dynamic_slice_in_dim(current, row_begin, NB, 0)
            factor_rows = lax.dynamic_slice_in_dim(factor, (row_begin - next_start).astype(jnp.int32), NB, 0)
            change = jnp.dot(factor_rows.astype(jnp.float32), upper_wide, preferred_element_type=jnp.float32)
            refreshed = (row_slab[:, next_start:].astype(jnp.float32) - change).astype(jnp.bfloat16)
            return lax.dynamic_update_slice_in_dim(current, row_slab.at[:, next_start:].set(refreshed), row_begin, 0)

        dense = lax.fori_loop(panel_step + 1, ROWS // NB, update_block, dense)
    return dense.reshape(matrix.shape)
```

```python
import functools

import jax
import jax.numpy as jnp
from jax import lax
from jax.experimental import pallas as pl
from jax.experimental.pallas import tpu as pltpu
from jax.sharding import PartitionSpec as P

MESH = pl.DeviceIdType.MESH
TREES = (
    1672, 6666386, 4867713, 2995995, 7311392, 13313154, 11448897, 5972163,
    9641992, 11515034, 9660058, 7845587, 11972616, 13845514, 12048003, 10176200,
    14303752, 16176264, 14378632, 12505288, 11915848, 13788296, 11990665, 10117848,
    9527880, 11400339, 9660058, 7730906, 7139916, 13198417, 7720961, 5859033,
)
NB = 512
PIECES = 2
HOP = 2
GAP = 3


def exchange_kernel(
    panel, f_ref, g_ref, o_ref, l_ref, t_ref, oo_ref, fo_ref, a_buf, h_buf, b_buf,
    tree_recv, tree_send, a_sem, b_send, b_recv, c_send, c_recv, d_send, d_recv,
    o_recv, o_next, o_side, q_recv, q_next, q_side, q_home,
):
    prow = lax.axis_index("prow")
    pcol = lax.axis_index("pcol")
    x, core = prow // 2, prow % 2
    z, y = pcol // 4, pcol % 4
    root_x, root_core = panel // 2 % 4, panel % 2
    other = x * 2 + (1 - core)
    place = (z + 8 - panel // 4) % 8 * 4 + (y + 4 - panel % 4) % 4
    code = jnp.int32(TREES[0])
    for i in range(1, 32):
        code = jnp.where(place == i, jnp.int32(TREES[i]), code)
    tree_of = [code // 8**i % 8 for i in range(4)]
    begin = [code // 8 ** (4 + i) % 8 * HOP for i in range(4)]
    plane = [(z + 1) % 8 * 4 + y, (z + 7) % 8 * 4 + y, z * 4 + (y + 1) % 4, z * 4 + (y + 3) % 4]
    blocks = f_ref.shape[0] // NB
    rows = 128 // PIECES
    count = blocks * PIECES

    barrier = pltpu.get_barrier_semaphore()
    for d in range(4):
        pl.semaphore_signal(barrier, inc=1, device_id={"pcol": plane[d]}, device_id_type=MESH)
    for step in (1, 2, 3):
        pl.semaphore_signal(
            barrier, inc=1, device_id={"prow": (x + step) % 4 * 2 + core}, device_id_type=MESH
        )
    pl.semaphore_signal(barrier, inc=1, device_id={"prow": other}, device_id_type=MESH)
    pl.semaphore_wait(barrier, 8)

    def piece(t, j):
        start = j // PIECES * NB + t * 128 + j % PIECES * rows
        return pl.ds(pl.multiple_of(start, rows), rows)

    def tree_copy(t, j, d):
        at = piece(t, j)
        return pltpu.make_async_remote_copy(
            src_ref=l_ref.at[at], dst_ref=l_ref.at[at], send_sem=tree_send.at[d, j],
            recv_sem=tree_recv.at[t, j], device_id={"pcol": plane[d]}, device_id_type=MESH,
        )

    half = NB // 2
    quarter = half // 4
    mine = pl.ds(pl.multiple_of(core * half, half), half)
    theirs = pl.ds(pl.multiple_of((1 - core) * half, half), half)
    a_copy = pltpu.make_async_remote_copy(
        src_ref=g_ref.at[theirs], dst_ref=a_buf, send_sem=a_sem.at[0], recv_sem=a_sem.at[1],
        device_id={"prow": other}, device_id_type=MESH,
    )

    def b_copy(step):
        to = (x + step) % 4
        return pltpu.make_async_remote_copy(
            src_ref=h_buf.at[pl.ds(pl.multiple_of(to * quarter, quarter), quarter)],
            dst_ref=b_buf.at[step - 1], send_sem=b_send.at[step - 1], recv_sem=b_recv.at[step - 1],
            device_id={"prow": to * 2 + core}, device_id_type=MESH,
        )

    def summed(chip):
        return pl.ds(pl.multiple_of(core * half + chip * quarter, quarter), quarter)

    def c_copy(step):
        return pltpu.make_async_remote_copy(
            src_ref=t_ref.at[summed(x)], dst_ref=t_ref.at[summed(x)], send_sem=c_send.at[step - 1],
            recv_sem=c_recv.at[step - 1], device_id={"prow": (x + step) % 4 * 2 + core}, device_id_type=MESH,
        )

    def d_copy(step):
        chip = (x + 4 - step) % 4
        return pltpu.make_async_remote_copy(
            src_ref=t_ref.at[summed(chip)], dst_ref=t_ref.at[summed(chip)], send_sem=d_send.at[step],
            recv_sem=d_recv.at[step], device_id={"prow": other}, device_id_type=MESH,
        )

    far = [(x + 4 - root_x) % 4, (root_x + 4 - x) % 4]
    ahead = [(x + 1) % 4 * 2 + core, (x + 3) % 4 * 2 + core]
    on_chain = core == root_core

    def chain_copy(ref, h, c, recv, send, to):
        at = pl.ds(h * 256 + c * 128, 128)
        return pltpu.make_async_remote_copy(
            src_ref=ref.at[at], dst_ref=ref.at[at], send_sem=send.at[h, c], recv_sem=recv.at[h, c],
            device_id={"prow": to}, device_id_type=MESH,
        )

    def arrival(ref, at, sem):
        return pltpu.make_async_copy(ref.at[at], ref.at[at], sem)

    def chain_step(ref, h, c, recv, forward, side):
        arrival(ref, pl.ds(h * 256 + c * 128, 128), recv.at[h, c]).wait()

        @pl.when(far[h] < 3)
        def _():
            chain_copy(ref, h, c, recv, forward, ahead[h]).start()

        chain_copy(ref, h, c, recv, side, other).start()

    a_copy.start()

    @pl.when(place == 0)
    def _():
        @pl.loop(0, count)
        def _(j):
            for t in range(4):
                pltpu.make_async_copy(f_ref.at[piece(t, j)], l_ref.at[piece(t, j)], tree_recv.at[t, j]).start()

    @pl.when(on_chain & (x == root_x))
    def _():
        for h in range(2):
            for c in range(2):
                at = pl.ds(h * 256 + c * 128, 128)
                pltpu.make_async_copy(o_ref.at[at], oo_ref.at[at], o_recv.at[h, c]).start()

    top_done = begin[0]
    for t in range(1, 4):
        top_done = jnp.maximum(top_done, begin[t])
    top_done = top_done + PIECES
    total = max(count + 7 * HOP, 7 * HOP + PIECES + 3 * GAP + 3)

    @pl.loop(0, total)
    def _(s):
        for t in range(4):
            j = s - begin[t]

            @pl.when((j >= 0) & (j < count))
            def _():
                arrival(l_ref, piece(t, j), tree_recv.at[t, j]).wait()
                for d in range(4):
                    @pl.when(tree_of[d] == t)
                    def _():
                        tree_copy(t, j, d).start()

        @pl.when(s == 1)
        def _():
            a_copy.wait_recv()
            h_buf[...] = g_ref[mine, :] + a_buf[...]

        @pl.when(s == 2)
        def _():
            for step in (2, 1, 3):
                b_copy(step).start()

        @pl.when(s == 9)
        def _():
            for step in (1, 2, 3):
                b_copy(step).wait_recv()
            own = h_buf[pl.ds(pl.multiple_of(x * quarter, quarter), quarter), :]
            t_ref[summed(x), :] = own + b_buf[0] + (b_buf[1] + b_buf[2])

        @pl.when(s == 10)
        def _():
            for step in (2, 1, 3):
                c_copy(step).start()
            d_copy(0).start()

        @pl.when(s == 17)
        def _():
            for step in (1, 3, 2):
                c_copy(step).wait_recv()
                d_copy(step).start()

        for h in range(2):
            for c in range(2):
                @pl.when(on_chain & (s == 1 + GAP * far[h] + 2 * c))
                def _():
                    chain_step(oo_ref, h, c, o_recv, o_next, o_side)

        @pl.when((prow == panel % 8) & (s == top_done))
        def _():
            for h in range(2):
                for c in range(2):
                    at = pl.ds(h * 256 + c * 128, 128)
                    pltpu.make_async_copy(l_ref.at[at], fo_ref.at[at], q_recv.at[h, c]).start()

        for h in range(2):
            for c in range(2):
                @pl.when(on_chain & (s == top_done + GAP * far[h] + c))
                def _():
                    chain_step(fo_ref, h, c, q_recv, q_next, q_side)

    @pl.loop(0, count)
    def _(j):
        for d in range(4):
            @pl.when(tree_of[d] < 4)
            def _():
                tree_copy(0, j, d).wait_send()

    a_copy.wait_send()
    for step in (1, 2, 3):
        b_copy(step).wait_send()
        c_copy(step).wait_send()
    for step in range(4):
        d_copy(step).wait()
    for ref, recv, forward, side in ((oo_ref, o_recv, o_next, o_side), (fo_ref, q_recv, q_next, q_side)):
        for h in range(2):
            for c in range(2):
                @pl.when(on_chain)
                def _():
                    chain_copy(ref, h, c, recv, side, other).wait_send()

                @pl.when(on_chain & (far[h] < 3))
                def _():
                    chain_copy(ref, h, c, recv, forward, ahead[h]).wait_send()

                @pl.when(core != root_core)
                def _():
                    arrival(ref, pl.ds(h * 256 + c * 128, 128), recv.at[h, c]).wait()


def exchange(panel, factor, picked, top):
    rows, width = factor.shape[0], picked.shape[1]
    vmem = pl.BlockSpec(memory_space=pltpu.VMEM)
    count = rows // NB * PIECES
    dma = pltpu.SemaphoreType.DMA
    return pl.pallas_call(
        functools.partial(exchange_kernel, panel),
        out_shape=(
            jax.ShapeDtypeStruct((rows, NB), jnp.bfloat16),
            jax.ShapeDtypeStruct((NB, width), jnp.bfloat16),
            jax.ShapeDtypeStruct((NB, width), jnp.bfloat16),
            jax.ShapeDtypeStruct((NB, NB), jnp.bfloat16),
        ),
        in_specs=[vmem] * 3,
        out_specs=(vmem,) * 4,
        scratch_shapes=[
            pltpu.VMEM((NB // 2, width), jnp.bfloat16),
            pltpu.VMEM((NB // 2, width), jnp.bfloat16),
            pltpu.VMEM((3, NB // 8, width), jnp.bfloat16),
            dma((4, count)), dma((4, count)), dma((2,)), dma((3,)), dma((3,)), dma((3,)), dma((3,)),
            dma((4,)), dma((4,)),
            dma((2, 2)), dma((2, 2)), dma((2, 2)), dma((2, 2)), dma((2, 2)), dma((2, 2)), dma((2, 2)),
        ],
        compiler_params=pltpu.CompilerParams(
            collective_id=panel, has_side_effects=True, vmem_limit_bytes=48 << 20
        ),
        name=f"exchange{panel}",
    )(factor, picked, top)


def dot(a, b):
    return jnp.dot(a, b, preferred_element_type=jnp.float32)


def pick(place_ref, wanted_ref, tiles_ref, hot_ref, g_ref):
    rows, width = tiles_ref.shape
    my_row = place_ref[0]

    @pl.loop(0, rows // NB)
    def _(i):
        held = (i * 8 + my_row) * NB + lax.broadcasted_iota(jnp.int32, (1, NB), 1)
        at = pl.ds(pl.multiple_of(i * NB, NB), NB)
        hot_ref[:, at] = jnp.where(wanted_ref[...] == held, 1.0, 0.0).astype(jnp.bfloat16)

    @pl.loop(0, width // 256)
    def _(i):
        at = pl.ds(pl.multiple_of(i * 256, 256), 256)
        g_ref[:, at] = dot(hot_ref[...], tiles_ref[:, at]).astype(jnp.bfloat16)


def scale(tiles_ref, upper_ref, f_ref):
    @pl.loop(0, tiles_ref.shape[0] // 256)
    def _(i):
        at = pl.ds(pl.multiple_of(i * 256, 256), 256)
        f_ref[at, :] = dot(tiles_ref[at, :NB], upper_ref[...]).astype(jnp.bfloat16)


def first_kernel(place_ref, wanted_ref, tiles_ref, upper_ref, f_ref, g_ref, hot_ref):
    scale(tiles_ref, upper_ref, f_ref)
    pick(place_ref, wanted_ref, tiles_ref, hot_ref, g_ref)


def update_kernel(
    panel, last, place_ref, piv_ref, tiles_ref, l_ref, t_ref, oo_ref, fo_ref, lower_ref, *rest
):
    if last:
        out_ref, u_ref, w_ref, top_ref = rest
    else:
        wanted_ref, upper_ref, out_ref, f_ref, g_ref, u_ref, w_ref, top_ref, hot_ref = rest
    my_row, my_col = place_ref[0], place_ref[1]
    next_start = (panel + 1) * NB
    rows, width = tiles_ref.shape

    for i in range(width // NB):
        at = slice(i * NB, (i + 1) * NB)
        product = dot(lower_ref[...], t_ref[:, at]).astype(jnp.bfloat16)
        u_ref[:, at] = product
        top_ref[:, at] = product
        w_ref[:, at] = (oo_ref[:, at].astype(jnp.float32) - dot(fo_ref[...], product)).astype(jnp.bfloat16)

    @pl.when(my_col <= panel)
    def _():
        u_ref[:, :NB] = jnp.zeros((NB, NB), jnp.bfloat16)
        top_ref[:, :NB] = t_ref[:, :NB]
        w_ref[:, :NB] = oo_ref[:, :NB]

    @pl.when(my_col == panel)
    def _():
        w_ref[:, :NB] = fo_ref[...]

    piv = piv_ref[...]
    swapped = piv >= next_start

    @pl.loop(0, rows // 256)
    def _(i):
        at = pl.ds(pl.multiple_of(i * 256, 256), 256)
        base = (i // 2 * 8 + my_row) * NB + i % 2 * 256
        held = base + lax.broadcasted_iota(jnp.int32, (256, 1), 0)
        hot = jnp.where((held == piv) & swapped, 1.0, 0.0)
        moved = jnp.max(hot, axis=1, keepdims=True) > 0.0
        hot = hot.astype(jnp.bfloat16)
        factor = l_ref[at, :]
        for c in range(width // NB):
            cols = slice(c * NB, (c + 1) * NB)
            old = tiles_ref[at, cols]
            if c == 0:
                old = jnp.where(my_col == panel, factor, old)
            fresh = old.astype(jnp.float32) - dot(factor, u_ref[:, cols])
            out_ref[at, cols] = jnp.where(moved, dot(hot, w_ref[:, cols]), fresh).astype(jnp.bfloat16)

    @pl.when(my_row == panel % 8)
    def _():
        out_ref[:NB, :] = top_ref[...]

    @pl.when(my_row < panel)
    def _():
        out_ref[:NB, :] = tiles_ref[:NB, :]

    if not last:
        scale(out_ref, upper_ref, f_ref)
        pick(place_ref, wanted_ref, out_ref, hot_ref, g_ref)


VMEM = pl.BlockSpec(memory_space=pltpu.VMEM)
SMEM = pl.BlockSpec(memory_space=pltpu.SMEM)
PARAMS = pltpu.CompilerParams(vmem_limit_bytes=56 << 20)


def body(matrix, pivots, lower_inverse, upper_inverse):
    row_blocks, block_width, col_blocks, _ = matrix.shape
    rows, width = row_blocks * block_width, col_blocks * block_width
    steps_count = pivots.shape[0]
    place = jnp.stack([lax.axis_index("prow"), lax.axis_index("pcol")]).astype(jnp.int32)
    tiles = matrix.reshape(rows, width)
    half = functools.partial(jax.ShapeDtypeStruct, dtype=jnp.bfloat16)
    factor, picked = pl.pallas_call(
        first_kernel,
        out_shape=(half((rows, NB)), half((NB, width))),
        in_specs=[SMEM, VMEM, VMEM, VMEM],
        out_specs=(VMEM, VMEM),
        scratch_shapes=[pltpu.VMEM((NB, rows), jnp.bfloat16)],
        compiler_params=PARAMS,
        name="first",
    )(place, pivots[0][:, None], tiles, upper_inverse[0])
    for panel in range(steps_count):
        last = panel == steps_count - 1
        spread, picked_all, top_all, top_factor = exchange(panel, factor, picked, tiles[:NB])
        operands = [place, pivots[panel][None, :], tiles, spread, picked_all, top_all, top_factor,
                    lower_inverse[panel]]
        out_shape = [half((rows, width))]
        scratch = [pltpu.VMEM((NB, width), jnp.bfloat16)] * 3
        if not last:
            operands += [pivots[panel + 1][:, None], upper_inverse[panel + 1]]
            out_shape += [half((rows, NB)), half((NB, width))]
            scratch += [pltpu.VMEM((NB, rows), jnp.bfloat16)]
        result = pl.pallas_call(
            functools.partial(update_kernel, panel, last),
            out_shape=tuple(out_shape),
            in_specs=[SMEM] + [VMEM] * (len(operands) - 1),
            out_specs=(VMEM,) * len(out_shape),
            scratch_shapes=scratch,
            compiler_params=PARAMS,
            name=f"update{panel}",
        )(*operands)
        tiles = result[0]
        if not last:
            factor, picked = result[1:]
    return tiles.reshape(matrix.shape)


def solution(mesh):
    placed = (P(None, "prow", None, "pcol"), P(), P(), P())
    return jax.shard_map(
        body, mesh=mesh, in_specs=placed, out_specs=P(None, "prow", None, "pcol"), check_vma=False
    )
```

```python
import functools

import jax
import jax.numpy as jnp
from jax import lax
from jax.experimental import pallas as pl
from jax.experimental.pallas import tpu as pltpu
from jax.sharding import PartitionSpec as P

MESH = pl.DeviceIdType.MESH
TREES = (
    1672, 6666386, 4867713, 2995995, 7311392, 13313154, 11448897, 5972163,
    9641992, 11515034, 9660058, 7845587, 11972616, 13845514, 12048003, 10176200,
    14303752, 16176264, 14378632, 12505288, 11915848, 13788296, 11990665, 10117848,
    9527880, 11400339, 9660058, 7730906, 7139916, 13198417, 7720961, 5859033,
)
NB = 512
PIECES = 4
HOP = 4
GAP = 7
CHAIN_AT = 14
EVERY = 3
SUM_AT = 4
SUM_GAP = 6
SUM_STEPS = (0, 1, 8, 9, 14, 15, 20, 27, 32)


def exchange_kernel(
    tiles_ref, g_ref, c0_ref, c1_ref, t_ref, o_ref, q_ref,
    a_buf, h_buf, b1_buf, b2_buf,
    recv0, recv1, send0, send1, a_send, a_recv, b1_send, b1_recv, b2_send, b2_recv,
    d1_send, d1_recv, d2_send, d2_recv, e_send, e_recv,
    o_recv, o_next, o_side, o_other, q_recv, q_next, q_side, q_other, q_home,
):
    prow = lax.axis_index("prow")
    pcol = lax.axis_index("pcol")
    x, core = prow // 2, prow % 2
    z, y = pcol // 4, pcol % 4
    other = x * 2 + (1 - core)
    plane = [(z + 1) % 8 * 4 + y, (z + 7) % 8 * 4 + y, z * 4 + (y + 1) % 4, z * 4 + (y + 3) % 4]
    rows = 128 // PIECES
    blocks = tiles_ref.shape[0] // NB
    p = PIECES
    count = (blocks + 1) * p

    def lookup(place):
        code = jnp.int32(TREES[0])
        for i in range(1, 32):
            code = jnp.where(place == i, jnp.int32(TREES[i]), code)
        tree_of = [code // 8**i % 8 for i in range(4)]
        begin = [code // 8 ** (4 + i) % 8 * HOP for i in range(4)]
        wait_at = [jnp.where(place == 0, 1000, at) for at in begin]
        send_at = []
        for tree in tree_of:
            at = jnp.where(tree == 0, begin[0], 1000)
            for i in range(1, 4):
                at = jnp.where(tree == i, begin[i], at)
            send_at.append(at)
        return tree_of, begin, wait_at, send_at

    place = [pcol, z * 4 + (y + 3) % 4]
    trees = [lookup(place[0]), lookup(place[1])]
    panels = [c0_ref, c1_ref]
    recvs, sends = [recv0, recv1], [send0, send1]

    pair = [(x + 1 - 2 * (x % 2)) * 2 + core, (3 - x) * 2 + core]
    bit = [(x + 1) // 2 % 2, x // 2]
    ahead = [(x + 1) % 4 * 2 + core, (x + 3) % 4 * 2 + core]

    barrier = pltpu.get_barrier_semaphore()
    for d in range(4):
        pl.semaphore_signal(barrier, inc=1, device_id={"pcol": plane[d]}, device_id_type=MESH)
    for to in ahead + [other]:
        pl.semaphore_signal(barrier, inc=1, device_id={"prow": to}, device_id_type=MESH)
    pl.semaphore_wait(barrier, 7)

    def remote(src, dst, send, recv, **to):
        return pltpu.make_async_remote_copy(
            src_ref=src, dst_ref=dst, send_sem=send, recv_sem=recv, device_id=to, device_id_type=MESH
        )

    def arrival(ref, sem):
        return pltpu.make_async_copy(ref, ref, sem)

    def piece(t, j):
        start = j // p * NB + t * 128 + j % p * rows
        return pl.ds(pl.multiple_of(start, rows), rows)

    def tree_copy(r, t, j, d):
        at = panels[r].at[piece(t, j)]
        return remote(at, at, sends[r].at[d, j], recvs[r].at[t, j], pcol=plane[d])

    def slot(r, u):
        if r == 0:
            valid = ((u >= 0) & (u < p)) | ((u >= 2 * p) & (u < 6 * p)) | ((u >= 10 * p) & (u < 11 * p))
            return valid, jnp.where(u < p, u, jnp.where(u < 6 * p, u - p, u - 5 * p))
        valid = ((u >= p) & (u < 2 * p)) | ((u >= 6 * p) & (u < 10 * p)) | ((u >= 11 * p) & (u < 12 * p))
        return valid, jnp.where(u < 2 * p, u - p, jnp.where(u < 10 * p, u - 5 * p, u - 6 * p))

    def tree_step(r, s):
        tree_of, begin, wait_at, send_at = trees[r]
        for t in range(4):
            due, j = slot(r, s - wait_at[t])

            @pl.when(due)
            def _():
                arrival(panels[r].at[piece(t, j)], recvs[r].at[t, j]).wait()

        for d in range(4):
            ready, i = slot(r, s - send_at[d])

            @pl.when(ready)
            def _():
                tree_copy(r, tree_of[d], i, d).start()

    def cols(h):
        return pl.ds(h * NB, NB)

    mine = pl.ds(pl.multiple_of(core * NB, NB), NB)
    theirs = pl.ds(pl.multiple_of((1 - core) * NB, NB), NB)

    def a_copy(h):
        return remote(g_ref.at[theirs, cols(h)], a_buf.at[h], a_send.at[h], a_recv.at[h], prow=other)

    def kept(e, sign):
        b = bit[e] if sign else 1 - bit[e]
        return pl.ds(pl.multiple_of(e * 256 + b * 128, 128), 128)

    def final(e, sign):
        b = bit[1 - e] if sign else 1 - bit[1 - e]
        return e * 256 + bit[e] * 128 + b * 64

    def b1_copy(h, e):
        return remote(h_buf.at[h, kept(e, False)], b1_buf.at[h, e], b1_send.at[h, e], b1_recv.at[h, e], prow=pair[e])

    def b2_copy(h, e):
        at = pl.ds(pl.multiple_of(final(e, False), 64), 64)
        return remote(h_buf.at[h, at], b2_buf.at[h, e], b2_send.at[h, e], b2_recv.at[h, e], prow=pair[1 - e])

    def d1_copy(h, e):
        ref = t_ref.at[pl.ds(pl.multiple_of(core * NB + final(e, True), 64), 64), cols(h)]
        return remote(ref, ref, d1_send.at[h, e], d1_recv.at[h, e], prow=pair[1 - e])

    def d2_copy(h, e):
        ref = t_ref.at[pl.ds(pl.multiple_of(core * NB + e * 256 + bit[e] * 128, 128), 128), cols(h)]
        return remote(ref, ref, d2_send.at[h, e], d2_recv.at[h, e], prow=pair[e])

    def e_copy(h):
        ref = t_ref.at[mine, cols(h)]
        return remote(ref, ref, e_send.at[h], e_recv.at[h], prow=other)

    def sum_step(h, k):
        if k == 0:
            a_copy(h).wait_recv()
            h_buf[h] = g_ref[mine, h * NB : (h + 1) * NB] + a_buf[h]
        elif k == 1:
            for e in range(2):
                b1_copy(h, e).start()
        elif k == 2:
            for e in range(2):
                b1_copy(h, e).wait_recv()
                h_buf[h, kept(e, True)] += b1_buf[h, e]
        elif k == 3:
            for e in range(2):
                b2_copy(h, e).start()
        elif k == 4:
            for e in range(2):
                b2_copy(h, e).wait_recv()
                at = final(e, True)
                t_ref[pl.ds(pl.multiple_of(core * NB + at, 64), 64), h * NB : (h + 1) * NB] = (
                    h_buf[h, pl.ds(pl.multiple_of(at, 64), 64)] + b2_buf[h, e]
                )
        elif k == 5:
            for e in range(2):
                d1_copy(h, e).start()
        elif k == 6:
            for e in range(2):
                d1_copy(h, e).wait_recv()
                d2_copy(h, e).start()
        elif k == 7:
            for e in range(2):
                d2_copy(h, e).wait_recv()
            e_copy(h).start()
        else:
            e_copy(h).wait_recv()

    far = [x, (4 - x) % 4]

    def link(h, c, of):
        return pl.ds(pl.multiple_of(of * NB + h * 256 + c * 64, 64), 64)

    def chain_send(ref, h, c, recv, forward):
        at = ref.at[link(h, c, core)]
        return remote(at, at, forward.at[h, c], recv.at[h, c], prow=ahead[h])

    def side_send(ref, h, c, side, opposite):
        at = ref.at[link(h, c, core)]
        return remote(at, at, side.at[h, c], opposite.at[h, c], prow=other)

    def chain_step(ref, h, c, recv, forward, side, opposite):
        arrival(ref.at[link(h, c, core)], recv.at[h, c]).wait()

        @pl.when(far[h] < 3)
        def _():
            chain_send(ref, h, c, recv, forward).start()

        side_send(ref, h, c, side, opposite).start()

    def home(h, c, i):
        at = pl.ds(h * 256 + c * 64, 64)
        return pltpu.make_async_copy(
            panels[i].at[at], q_ref.at[link(h, c, core), pl.ds(i * NB, NB)], q_home.at[h, c, i]
        )

    units = [(h, c) for h in range(2) for c in range(4)]

    for h in range(2):
        a_copy(h).start()

    @pl.when(x == 0)
    def _():
        for h, c in units:
            pltpu.make_async_copy(
                tiles_ref.at[pl.ds(h * 256 + c * 64, 64)], o_ref.at[link(h, c, core)], o_recv.at[h, c]
            ).start()

    for r in range(2):
        @pl.when(place[r] == 0)
        def _():
            own = pltpu.make_async_copy(
                tiles_ref.at[:, pl.ds(0, NB)], panels[r].at[pl.ds(0, blocks * NB)], a_send.at[2]
            )
            own.start()
            own.wait()

    top_at = 7 * HOP + 2 * p
    actions = {}

    def plan(step, action):
        actions.setdefault(step, []).append(action)

    for h in range(2):
        for k, at in enumerate(SUM_STEPS):
            plan(SUM_AT + at + SUM_GAP * h, functools.partial(sum_step, h, k))

    def root_rest():
        for r in range(2):
            @pl.when(place[r] == 0)
            def _():
                rest = pltpu.make_async_copy(
                    t_ref.at[pl.ds((1 - r) * NB, NB), pl.ds(0, NB)],
                    panels[r].at[pl.ds(blocks * NB, NB)], a_send.at[3],
                )
                rest.start()
                rest.wait()

    plan(max(SUM_AT + SUM_STEPS[-1], 0), root_rest)

    def old_rows(h, c, hop):
        @pl.when(far[h] == hop)
        def _():
            chain_step(o_ref, h, c, o_recv, o_next, o_side, o_other)

    def at_home():
        @pl.when(x == 0)
        def _():
            for h, c in units:
                for i in range(2):
                    home(h, c, i).start()

    def old_panels(h, c, hop):
        @pl.when(far[h] == hop)
        def _():
            if hop:
                chain_step(q_ref, h, c, q_recv, q_next, q_side, q_other)
            else:
                for i in range(2):
                    home(h, c, i).wait()
                chain_send(q_ref, h, c, q_recv, q_next).start()
                side_send(q_ref, h, c, q_side, q_other).start()

    for hop in range(4):
        for h, c in units:
            plan(CHAIN_AT + GAP * hop + EVERY * c, functools.partial(old_rows, h, c, hop))
            plan(top_at + 1 + GAP * hop + EVERY * c, functools.partial(old_panels, h, c, hop))
    plan(top_at, at_home)
    total = max(12 * p + 7 * HOP, max(actions) + 1)

    @pl.loop(0, total)
    def _(s):
        for r in range(2):
            tree_step(r, s)

        for first in range(0, total, 8):
            inside = [step for step in range(first, first + 8) if step in actions]
            if inside:
                @pl.when((s >= inside[0]) & (s <= inside[-1]))
                def _():
                    for step in inside:
                        @pl.when(s == step)
                        def _():
                            for action in actions[step]:
                                action()

    for r in range(2):
        tree_of = trees[r][0]

        @pl.loop(0, count)
        def _(j):
            for d in range(4):
                @pl.when(tree_of[d] < 4)
                def _():
                    tree_copy(r, 0, j, d).wait_send()

    for h in range(2):
        a_copy(h).wait_send()
        e_copy(h).wait_send()
        for e in range(2):
            for copy in (b1_copy, b2_copy, d1_copy, d2_copy):
                copy(h, e).wait_send()
    for ref, recv, forward, side, opposite in (
        (o_ref, o_recv, o_next, o_side, o_other), (q_ref, q_recv, q_next, q_side, q_other)
    ):
        for h, c in units:
            @pl.when(far[h] < 3)
            def _():
                chain_send(ref, h, c, recv, forward).wait_send()

            side_send(ref, h, c, side, opposite).wait_send()
            arrival(ref.at[link(h, c, 1 - core)], opposite.at[h, c]).wait()


def half(*shape):
    return jax.ShapeDtypeStruct(shape, jnp.bfloat16)


def exchange(tiles, picked):
    rows, width = tiles.shape
    vmem = pl.BlockSpec(memory_space=pltpu.VMEM)
    count = (rows // NB + 1) * PIECES
    dma = pltpu.SemaphoreType.DMA
    buf = functools.partial(pltpu.VMEM, dtype=jnp.bfloat16)
    return pl.pallas_call(
        exchange_kernel,
        out_shape=(half(rows + NB, NB), half(rows + NB, NB), half(2 * NB, width), half(2 * NB, width),
                   half(2 * NB, width)),
        in_specs=[pl.BlockSpec(memory_space=pl.ANY), vmem],
        out_specs=(vmem,) * 5,
        scratch_shapes=[buf((2, NB, NB)), buf((2, NB, NB)), buf((2, 2, 128, NB)), buf((2, 2, 64, NB)),
                        dma((4, count)), dma((4, count)), dma((4, count)), dma((4, count)),
                        dma((4,)), dma((2,))]
        + [dma((2, 2))] * 8 + [dma((2,))] * 2 + [dma((2, 4))] * 8 + [dma((2, 4, 2))],
        compiler_params=pltpu.CompilerParams(collective_id=0, has_side_effects=True, vmem_limit_bytes=48 << 20),
        name="exchange",
    )(tiles, picked)


def dot(a, b):
    return jnp.dot(a, b, preferred_element_type=jnp.float32)


def iota(shape, dim):
    return lax.broadcasted_iota(jnp.int32, shape, dim).astype(jnp.float32)


def pivot_vectors(piv_ref):
    rows = [piv_ref[i : i + 1, :].astype(jnp.float32) for i in range(2)]
    eye = iota((NB, NB), 0) == iota((NB, NB), 1)
    columns = [jnp.sum(jnp.where(eye, row, 0.0), axis=1, keepdims=True) for row in rows]
    return rows, columns


def pick_kernel(place_ref, piv_ref, tiles_ref, g_ref, hot_ref):
    rows, width = tiles_ref.shape
    my_row = place_ref[0].astype(jnp.float32)
    (row0, _), (col0, col1) = pivot_vectors(piv_ref)
    same = col1 == row0
    index = jnp.sum(jnp.where(same, iota((NB, NB), 1), 0.0), axis=1, keepdims=True)
    found = jnp.max(jnp.where(same, 1.0, 0.0), axis=1, keepdims=True) > 0.0
    second = jnp.where(found, index, col1)

    for i in range(rows // NB):
        held = (i * 8 + my_row) * NB + iota((1, NB), 1)
        at = slice(i * NB, (i + 1) * NB)
        hot_ref[:NB, at] = jnp.where(col0 == held, 1.0, 0.0).astype(jnp.bfloat16)
        hot_ref[NB:, at] = jnp.where(second == held, 1.0, 0.0).astype(jnp.bfloat16)

    @pl.loop(0, width // 256)
    def _(i):
        at = pl.ds(pl.multiple_of(i * 256, 256), 256)
        g_ref[:, at] = dot(hot_ref[...], tiles_ref[:, at]).astype(jnp.bfloat16)


def finish_kernel(
    place_ref, piv_ref, tiles_ref, c0_ref, c1_ref, t_ref, o_ref, q_ref, lower_ref, upper_ref, out_ref,
    u_ref, w_ref, top_ref,
):
    my_row, my_col = place_ref[0], place_ref[1]
    rows, width = tiles_ref.shape
    bf16 = jnp.bfloat16

    (row0, row1), (col0, col1) = pivot_vectors(piv_ref)
    into = iota((NB, NB), 0) + NB == row0
    also = col1 == row0
    down = jnp.sum(jnp.where(into, col1, 0.0), axis=0, keepdims=True)
    back = jnp.sum(jnp.where(also, iota((NB, NB), 0) + NB, 0.0), axis=0, keepdims=True)
    went = jnp.max(jnp.where(into, 1.0, 0.0), axis=0, keepdims=True) > 0.0
    came = jnp.max(jnp.where(also, 1.0, 0.0), axis=0, keepdims=True) > 0.0
    dest0 = jnp.where(went, down, jnp.where(came, back, row0))
    up = col0 == iota((1, NB), 1) + NB
    rose = jnp.max(jnp.where(up, 1.0, 0.0), axis=0, keepdims=True) > 0.0
    dest1 = jnp.where(rose, 0.0, row1)

    factor10 = dot(c0_ref[rows:, :], upper_ref[0]).astype(bf16)
    upper01 = dot(lower_ref[0], c1_ref[rows:, :]).astype(bf16)

    def factors(first, second):
        f0 = dot(first, upper_ref[0]).astype(bf16)
        rest = (second.astype(jnp.float32) - dot(f0, upper01)).astype(bf16)
        return f0, dot(rest, upper_ref[1]).astype(bf16)

    for i in range(width // NB):
        at = slice(i * NB, (i + 1) * NB)
        u0 = dot(lower_ref[0], t_ref[:NB, at]).astype(bf16)
        t1 = (t_ref[NB:, at].astype(jnp.float32) - dot(factor10, u0)).astype(bf16)
        u1 = dot(lower_ref[1], t1).astype(bf16)
        if i == 0:
            special0, special1 = my_col == 0, my_col == 1
            top_ref[:NB, at] = jnp.where(special0, t_ref[:NB, at], u0)
            top_ref[NB:, at] = jnp.where(special0, factor10, jnp.where(special1, t1, u1))
            u0 = jnp.where(special0 | special1, jnp.zeros_like(u0), u0)
            u1 = jnp.where(special0 | special1, jnp.zeros_like(u1), u1)
        else:
            top_ref[:NB, at] = u0
            top_ref[NB:, at] = u1
        u_ref[:NB, at] = u0
        u_ref[NB:, at] = u1

    def update(old, f0, f1, c):
        at = slice(c * NB, (c + 1) * NB)
        if c == 0:
            old = jnp.where(my_col == 0, f0, jnp.where(my_col == 1, f1, old))
        old = (old.astype(jnp.float32) - dot(f0, u_ref[:NB, at])).astype(bf16)
        return old.astype(jnp.float32) - dot(f1, u_ref[NB:, at])

    @pl.loop(0, 2 * NB // 256)
    def _(i):
        at = pl.ds(pl.multiple_of(i * 256, 256), 256)
        f0, f1 = factors(q_ref[at, :NB], q_ref[at, NB:])
        for c in range(width // NB):
            w_ref[at, c * NB : (c + 1) * NB] = update(o_ref[at, c * NB : (c + 1) * NB], f0, f1, c).astype(bf16)

    @pl.loop(0, rows // 256)
    def _(i):
        at = pl.ds(pl.multiple_of(i * 256, 256), 256)
        base = (i // 2 * 8 + my_row) * NB + i % 2 * 256
        held = base.astype(jnp.float32) + iota((256, 1), 0)
        hot0 = jnp.where(held == dest0, 1.0, 0.0)
        hot1 = jnp.where(held == dest1, 1.0, 0.0)
        moved = jnp.max(jnp.maximum(hot0, hot1), axis=1, keepdims=True) > 0.0
        hot0, hot1 = hot0.astype(bf16), hot1.astype(bf16)
        f0, f1 = factors(c0_ref[at, :], c1_ref[at, :])
        for c in range(width // NB):
            cols = slice(c * NB, (c + 1) * NB)
            fresh = update(tiles_ref[at, cols], f0, f1, c)
            placed = dot(hot0, w_ref[:NB, cols]) + dot(hot1, w_ref[NB:, cols])
            out_ref[at, cols] = jnp.where(moved, placed, fresh).astype(bf16)

    for r in range(2):
        @pl.when(my_row == r)
        def _():
            out_ref[:NB, :] = top_ref[r * NB : (r + 1) * NB, :]


VMEM = pl.BlockSpec(memory_space=pltpu.VMEM)
SMEM = pl.BlockSpec(memory_space=pltpu.SMEM)
PARAMS = pltpu.CompilerParams(vmem_limit_bytes=58 << 20)


def body(matrix, pivots, lower_inverse, upper_inverse):
    row_blocks, block_width, col_blocks, _ = matrix.shape
    rows, width = row_blocks * block_width, col_blocks * block_width
    place = jnp.stack([lax.axis_index("prow"), lax.axis_index("pcol")]).astype(jnp.int32)
    tiles = matrix.reshape(rows, width)
    picked = pl.pallas_call(
        pick_kernel,
        out_shape=half(2 * NB, width),
        in_specs=[SMEM, VMEM, VMEM],
        out_specs=VMEM,
        scratch_shapes=[pltpu.VMEM((2 * NB, rows), jnp.bfloat16)],
        compiler_params=PARAMS,
        name="pick",
    )(place, pivots, tiles)
    c0, c1, top_new, top_old, top_panels = exchange(tiles, picked)
    out = pl.pallas_call(
        finish_kernel,
        out_shape=half(rows, width),
        in_specs=[SMEM] + [VMEM] * 9,
        out_specs=VMEM,
        scratch_shapes=[pltpu.VMEM((2 * NB, width), jnp.bfloat16)] * 3,
        compiler_params=PARAMS,
        name="finish",
    )(place, pivots, tiles, c0, c1, top_new, top_old, top_panels, lower_inverse, upper_inverse)
    return out.reshape(matrix.shape)


def solution(mesh):
    placed = (P(None, "prow", None, "pcol"), P(), P(), P())
    return jax.shard_map(
        body, mesh=mesh, in_specs=placed, out_specs=P(None, "prow", None, "pcol"), check_vma=False
    )
```

```python
import functools

import jax
import jax.numpy as jnp
from jax import lax
from jax.experimental import pallas as pl
from jax.experimental.pallas import tpu as pltpu
from jax.sharding import PartitionSpec as P

MESH = pl.DeviceIdType.MESH
TREES = (
    1672, 6666386, 4867713, 2995995, 7311392, 13313154, 11448897, 5972163,
    9641992, 11515034, 9660058, 7845587, 11972616, 13845514, 12048003, 10176200,
    14303752, 16176264, 14378632, 12505288, 11915848, 13788296, 11990665, 10117848,
    9527880, 11400339, 9660058, 7730906, 7139916, 13198417, 7720961, 5859033,
)
NB = 512
PIECES = 2
HOP = 3
GAP = 5
EVERY = 1
CHAIN_AT = 14
SUM_AT = 1
SUM_GAP = 3
SUM_STEPS = (0, 1, 5, 6, 9, 10, 13, 16, 18)
GROUP = 256


def exchange_kernel(
    tiles_ref, g_ref, c0_ref, c1_ref, t_ref, o_ref, q_ref,
    a_buf, h_buf, b1_buf, b2_buf,
    recv0, recv1, send0, send1, a_send, a_recv, b1_send, b1_recv, b2_send, b2_recv,
    d1_send, d1_recv, d2_send, d2_recv, e_send, e_recv,
    o_recv, o_next, o_side, o_other, q_recv, q_next, q_side, q_other, q_home,
):
    prow = lax.axis_index("prow")
    pcol = lax.axis_index("pcol")
    x, core = prow // 2, prow % 2
    z, y = pcol // 4, pcol % 4
    other = x * 2 + (1 - core)
    plane = [(z + 1) % 8 * 4 + y, (z + 7) % 8 * 4 + y, z * 4 + (y + 1) % 4, z * 4 + (y + 3) % 4]
    rows = 128 // PIECES
    blocks = tiles_ref.shape[0] // NB
    p = PIECES
    count = (blocks + 1) * p

    def lookup(place):
        code = jnp.int32(TREES[0])
        for i in range(1, 32):
            code = jnp.where(place == i, jnp.int32(TREES[i]), code)
        tree_of = [code // 8**i % 8 for i in range(4)]
        begin = [code // 8 ** (4 + i) % 8 * HOP for i in range(4)]
        wait_at = [jnp.where(place == 0, 1000, at) for at in begin]
        send_at = []
        for tree in tree_of:
            at = jnp.where(tree == 0, begin[0], 1000)
            for i in range(1, 4):
                at = jnp.where(tree == i, begin[i], at)
            send_at.append(at)
        return tree_of, begin, wait_at, send_at

    place = [pcol, z * 4 + (y + 3) % 4]
    trees = [lookup(place[0]), lookup(place[1])]
    panels = [c0_ref, c1_ref]
    recvs, sends = [recv0, recv1], [send0, send1]

    pair = [(x + 1 - 2 * (x % 2)) * 2 + core, (3 - x) * 2 + core]
    bit = [(x + 1) // 2 % 2, x // 2]
    ahead = [(x + 1) % 4 * 2 + core, (x + 3) % 4 * 2 + core]

    barrier = pltpu.get_barrier_semaphore()
    for d in range(4):
        pl.semaphore_signal(barrier, inc=1, device_id={"pcol": plane[d]}, device_id_type=MESH)
    for to in ahead + [other]:
        pl.semaphore_signal(barrier, inc=1, device_id={"prow": to}, device_id_type=MESH)
    pl.semaphore_wait(barrier, 7)

    def remote(src, dst, send, recv, **to):
        return pltpu.make_async_remote_copy(
            src_ref=src, dst_ref=dst, send_sem=send, recv_sem=recv, device_id=to, device_id_type=MESH
        )

    def arrival(ref, sem):
        return pltpu.make_async_copy(ref, ref, sem)

    def piece(t, j):
        start = j // p * NB + t * 128 + j % p * rows
        return pl.ds(pl.multiple_of(start, rows), rows)

    def tree_copy(r, t, j, d):
        at = panels[r].at[piece(t, j)]
        return remote(at, at, sends[r].at[d, j], recvs[r].at[t, j], pcol=plane[d])

    def slot(r, u):
        return (u >= 0) & (u < 2 * count) & (u % 2 == r), u // 2

    def tree_step(r, s):
        tree_of, begin, wait_at, send_at = trees[r]
        for t in range(4):
            due, j = slot(r, s - wait_at[t])

            @pl.when(due)
            def _():
                arrival(panels[r].at[piece(t, j)], recvs[r].at[t, j]).wait()

        for d in range(4):
            ready, i = slot(r, s - send_at[d])

            @pl.when(ready)
            def _():
                tree_copy(r, tree_of[d], i, d).start()

    def cols(h):
        return pl.ds(h * NB, NB)

    mine = pl.ds(pl.multiple_of(core * NB, NB), NB)
    theirs = pl.ds(pl.multiple_of((1 - core) * NB, NB), NB)

    def a_copy(h):
        return remote(g_ref.at[theirs, cols(h)], a_buf.at[h], a_send.at[h], a_recv.at[h], prow=other)

    def kept(e, sign):
        b = bit[e] if sign else 1 - bit[e]
        return pl.ds(pl.multiple_of(e * 256 + b * 128, 128), 128)

    def final(e, sign):
        b = bit[1 - e] if sign else 1 - bit[1 - e]
        return e * 256 + bit[e] * 128 + b * 64

    def b1_copy(h, e):
        return remote(h_buf.at[h, kept(e, False)], b1_buf.at[h, e], b1_send.at[h, e], b1_recv.at[h, e], prow=pair[e])

    def b2_copy(h, e):
        at = pl.ds(pl.multiple_of(final(e, False), 64), 64)
        return remote(h_buf.at[h, at], b2_buf.at[h, e], b2_send.at[h, e], b2_recv.at[h, e], prow=pair[1 - e])

    def d1_copy(h, e):
        ref = t_ref.at[pl.ds(pl.multiple_of(core * NB + final(e, True), 64), 64), cols(h)]
        return remote(ref, ref, d1_send.at[h, e], d1_recv.at[h, e], prow=pair[1 - e])

    def d2_copy(h, e):
        ref = t_ref.at[pl.ds(pl.multiple_of(core * NB + e * 256 + bit[e] * 128, 128), 128), cols(h)]
        return remote(ref, ref, d2_send.at[h, e], d2_recv.at[h, e], prow=pair[e])

    def e_copy(h):
        ref = t_ref.at[mine, cols(h)]
        return remote(ref, ref, e_send.at[h], e_recv.at[h], prow=other)

    def sum_step(h, k):
        if k == 0:
            a_copy(h).wait_recv()
            h_buf[h] = g_ref[mine, h * NB : (h + 1) * NB] + a_buf[h]
        elif k == 1:
            for e in range(2):
                b1_copy(h, e).start()
        elif k == 2:
            for e in range(2):
                b1_copy(h, e).wait_recv()
                h_buf[h, kept(e, True)] += b1_buf[h, e]
        elif k == 3:
            for e in range(2):
                b2_copy(h, e).start()
        elif k == 4:
            for e in range(2):
                b2_copy(h, e).wait_recv()
                at = final(e, True)
                t_ref[pl.ds(pl.multiple_of(core * NB + at, 64), 64), h * NB : (h + 1) * NB] = (
                    h_buf[h, pl.ds(pl.multiple_of(at, 64), 64)] + b2_buf[h, e]
                )
        elif k == 5:
            for e in range(2):
                d1_copy(h, e).start()
        elif k == 6:
            for e in range(2):
                d1_copy(h, e).wait_recv()
                d2_copy(h, e).start()
        elif k == 7:
            for e in range(2):
                d2_copy(h, e).wait_recv()
            e_copy(h).start()
        else:
            e_copy(h).wait_recv()

    far = [x, (4 - x) % 4]

    def link(h, c, of):
        return pl.ds(pl.multiple_of(of * NB + h * 256 + c * 64, 64), 64)

    def chain_send(ref, h, c, recv, forward):
        at = ref.at[link(h, c, core)]
        return remote(at, at, forward.at[h, c], recv.at[h, c], prow=ahead[h])

    def side_send(ref, h, c, side, opposite):
        at = ref.at[link(h, c, core)]
        return remote(at, at, side.at[h, c], opposite.at[h, c], prow=other)

    def chain_step(ref, h, c, recv, forward, side, opposite):
        arrival(ref.at[link(h, c, core)], recv.at[h, c]).wait()

        @pl.when(far[h] < 3)
        def _():
            chain_send(ref, h, c, recv, forward).start()

        side_send(ref, h, c, side, opposite).start()

    def home(h, c, i):
        at = pl.ds(h * 256 + c * 64, 64)
        return pltpu.make_async_copy(
            panels[i].at[at], q_ref.at[link(h, c, core), pl.ds(i * NB, NB)], q_home.at[h, c, i]
        )

    units = [(h, c) for h in range(2) for c in range(4)]

    for h in range(2):
        a_copy(h).start()

    @pl.when(x == 0)
    def _():
        for h, c in units:
            pltpu.make_async_copy(
                tiles_ref.at[pl.ds(h * 256 + c * 64, 64)], o_ref.at[link(h, c, core)], o_recv.at[h, c]
            ).start()

    for r in range(2):
        @pl.when(place[r] == 0)
        def _():
            own = pltpu.make_async_copy(
                tiles_ref.at[:, pl.ds(0, NB)], panels[r].at[pl.ds(0, blocks * NB)], a_send.at[2]
            )
            own.start()
            own.wait()

    top_at = 7 * HOP + 2 * p
    actions = {}

    def plan(step, action):
        actions.setdefault(step, []).append(action)

    for h in range(2):
        for k, at in enumerate(SUM_STEPS):
            plan(SUM_AT + at + SUM_GAP * h, functools.partial(sum_step, h, k))

    def root_rest():
        for r in range(2):
            @pl.when(place[r] == 0)
            def _():
                rest = pltpu.make_async_copy(
                    t_ref.at[pl.ds((1 - r) * NB, NB), pl.ds(0, NB)],
                    panels[r].at[pl.ds(blocks * NB, NB)], a_send.at[3],
                )
                rest.start()
                rest.wait()

    assert SUM_AT + SUM_STEPS[-1] < 2 * blocks * p
    plan(SUM_AT + SUM_STEPS[-1], root_rest)

    def old_rows(h, c, hop):
        @pl.when(far[h] == hop)
        def _():
            chain_step(o_ref, h, c, o_recv, o_next, o_side, o_other)

    def at_home():
        @pl.when(x == 0)
        def _():
            for h, c in units:
                for i in range(2):
                    home(h, c, i).start()

    def old_panels(h, c, hop):
        @pl.when(far[h] == hop)
        def _():
            if hop:
                chain_step(q_ref, h, c, q_recv, q_next, q_side, q_other)
            else:
                for i in range(2):
                    home(h, c, i).wait()
                chain_send(q_ref, h, c, q_recv, q_next).start()
                side_send(q_ref, h, c, q_side, q_other).start()

    for hop in range(4):
        for h, c in units:
            plan(CHAIN_AT + GAP * hop + EVERY * c, functools.partial(old_rows, h, c, hop))
            plan(top_at + 1 + GAP * hop + EVERY * c, functools.partial(old_panels, h, c, hop))
    plan(top_at, at_home)
    total = max(2 * count + 7 * HOP, max(actions) + 1)

    @pl.loop(0, total)
    def _(s):
        for r in range(2):
            tree_step(r, s)

        for first in range(0, total, 8):
            inside = [step for step in range(first, first + 8) if step in actions]
            if inside:
                @pl.when((s >= inside[0]) & (s <= inside[-1]))
                def _():
                    for step in inside:
                        @pl.when(s == step)
                        def _():
                            for action in actions[step]:
                                action()

    for r in range(2):
        tree_of = trees[r][0]

        @pl.loop(0, count)
        def _(j):
            for d in range(4):
                @pl.when(tree_of[d] < 4)
                def _():
                    tree_copy(r, 0, j, d).wait_send()

    for h in range(2):
        a_copy(h).wait_send()
        e_copy(h).wait_send()
        for e in range(2):
            for copy in (b1_copy, b2_copy, d1_copy, d2_copy):
                copy(h, e).wait_send()
    for ref, recv, forward, side, opposite in (
        (o_ref, o_recv, o_next, o_side, o_other), (q_ref, q_recv, q_next, q_side, q_other)
    ):
        for h, c in units:
            @pl.when(far[h] < 3)
            def _():
                chain_send(ref, h, c, recv, forward).wait_send()

            side_send(ref, h, c, side, opposite).wait_send()
            arrival(ref.at[link(h, c, 1 - core)], opposite.at[h, c]).wait()


def half(*shape):
    return jax.ShapeDtypeStruct(shape, jnp.bfloat16)


def exchange(tiles, picked):
    rows, width = tiles.shape
    vmem = pl.BlockSpec(memory_space=pltpu.VMEM)
    count = (rows // NB + 1) * PIECES
    dma = pltpu.SemaphoreType.DMA
    buf = functools.partial(pltpu.VMEM, dtype=jnp.bfloat16)
    return pl.pallas_call(
        exchange_kernel,
        out_shape=(half(rows + NB, NB), half(rows + NB, NB), half(2 * NB, width), half(2 * NB, width),
                   half(2 * NB, width)),
        in_specs=[pl.BlockSpec(memory_space=pl.ANY), vmem],
        out_specs=(vmem,) * 5,
        scratch_shapes=[buf((2, NB, NB)), buf((2, NB, NB)), buf((2, 2, 128, NB)), buf((2, 2, 64, NB)),
                        dma((4, count)), dma((4, count)), dma((4, count)), dma((4, count)),
                        dma((4,)), dma((2,))]
        + [dma((2, 2))] * 8 + [dma((2,))] * 2 + [dma((2, 4))] * 8 + [dma((2, 4, 2))],
        compiler_params=pltpu.CompilerParams(collective_id=0, has_side_effects=True, vmem_limit_bytes=48 << 20),
        name="exchange",
    )(tiles, picked)


def dot(a, b):
    return jnp.dot(a, b, preferred_element_type=jnp.float32)


def iota(shape, dim):
    return lax.broadcasted_iota(jnp.int32, shape, dim).astype(jnp.float32)


def upright(row):
    n = row.shape[1]
    return jnp.sum(jnp.where(iota((n, n), 0) == iota((n, n), 1), row, 0.0), axis=1, keepdims=True)


def flat(column):
    n = column.shape[0]
    return jnp.sum(jnp.where(iota((n, n), 0) == iota((n, n), 1), column, 0.0), axis=0, keepdims=True)


def pivot_vectors(piv_ref):
    rows = [piv_ref[i : i + 1, :].astype(jnp.float32) for i in range(2)]
    return rows, [upright(row) for row in rows]


def ranks(targets, my_row, least):
    before = jnp.where(iota((NB, NB), 0) < iota((NB, NB), 1), 1.0, 0.0).astype(jnp.bfloat16)
    owned, places, total = [], [], 0.0
    for target in targets:
        whole = target.astype(jnp.int32)
        held = jnp.where((whole // NB % 8 == my_row) & (whole >= least), 1.0, 0.0)
        ahead = dot(jnp.broadcast_to(held, (16, NB)).astype(jnp.bfloat16), before)[:1]
        owned.append(held > 0.0)
        places.append(ahead + total)
        total = total + jnp.sum(held)
    groups = (total.astype(jnp.int32) + GROUP - 1) // GROUP
    return owned, places, groups


def choose(owned, place, group):
    slot = iota((GROUP, 1), 0) + (group * GROUP).astype(jnp.float32)
    return jnp.where(owned & (place == slot), 1.0, 0.0)


def pick_kernel(place_ref, piv_ref, tiles_ref, g_ref, hot_ref, few_ref, many_ref):
    rows, width = tiles_ref.shape
    my_row = place_ref[0]
    (row0, row1), (col0, _) = pivot_vectors(piv_ref)
    same = col0 == row1
    index = jnp.sum(jnp.where(same, iota((NB, NB), 0), 0.0), axis=0, keepdims=True)
    found = jnp.max(jnp.where(same, 1.0, 0.0), axis=0, keepdims=True) > 0.0
    sources = [row0, jnp.where(found, index, row1)]
    owned, places, groups = ranks(sources, my_row, 0)
    tall = [upright(jnp.where(have, place, -1.0)) for have, place in zip(owned, places)]

    def one_group(group, first):
        wanted = jnp.full((GROUP, 1), -1.0)
        for source, have, place in zip(sources, owned, places):
            wanted = wanted + jnp.sum(choose(have, place, group) * (source + 1.0), axis=1, keepdims=True)
        for i in range(rows // NB):
            held = ((i * 8 + my_row) * NB).astype(jnp.float32) + iota((1, NB), 1)
            hot_ref[:, i * NB : (i + 1) * NB] = jnp.where(wanted == held, 1.0, 0.0).astype(jnp.bfloat16)
        slot = iota((1, GROUP), 1) + (group * GROUP).astype(jnp.float32)
        for i in range(2):
            many_ref[i * NB : (i + 1) * NB, :] = jnp.where(tall[i] == slot, 1.0, 0.0).astype(jnp.bfloat16)

        @pl.loop(0, width // 256)
        def _(i):
            at = pl.ds(pl.multiple_of(i * 256, 256), 256)
            few_ref[...] = dot(hot_ref[...], tiles_ref[:, at]).astype(jnp.bfloat16)
            spread = dot(many_ref[...], few_ref[...])
            if not first:
                spread = spread + g_ref[:, at].astype(jnp.float32)
            g_ref[:, at] = spread.astype(jnp.bfloat16)

    one_group(jnp.int32(0), True)

    @pl.loop(1, groups)
    def _(group):
        one_group(group, False)


def finish_kernel(
    place_ref, piv_ref, tiles_ref, c0_ref, c1_ref, n0_ref, n1_ref, t_ref, o_ref, q_ref, lower_ref, upper_ref,
    out_ref, u_ref, w_ref, top_ref, u01_ref, row_ref, groups_ref,
):
    my_row, my_col = place_ref[0], place_ref[1]
    step = pl.program_id(0)
    rows, width = tiles_ref.shape
    bf16 = jnp.bfloat16

    def factors(first, second):
        f0 = dot(first, upper_ref[0]).astype(bf16)
        rest = (second.astype(jnp.float32) - dot(f0, u01_ref[...])).astype(bf16)
        return f0, dot(rest, upper_ref[1]).astype(bf16)

    def update(old, f0, f1, c):
        at = slice(c * NB, (c + 1) * NB)
        if c == 0:
            old = jnp.where(my_col == 0, f0, jnp.where(my_col == 1, f1, old))
        old = (old.astype(jnp.float32) - dot(f0, u_ref[:NB, at])).astype(bf16)
        return old.astype(jnp.float32) - dot(f1, u_ref[NB:, at])

    @pl.when(step == 0)
    def _():
        (row0, row1), (col0, col1) = pivot_vectors(piv_ref)
        into = iota((NB, NB), 0) + NB == row0
        also = col1 == row0
        down = jnp.sum(jnp.where(into, col1, 0.0), axis=0, keepdims=True)
        back = jnp.sum(jnp.where(also, iota((NB, NB), 0) + NB, 0.0), axis=0, keepdims=True)
        went = jnp.max(jnp.where(into, 1.0, 0.0), axis=0, keepdims=True) > 0.0
        came = jnp.max(jnp.where(also, 1.0, 0.0), axis=0, keepdims=True) > 0.0
        dest0 = jnp.where(went, down, jnp.where(came, back, row0))
        up = col0 == iota((1, NB), 1) + NB
        rose = jnp.max(jnp.where(up, 1.0, 0.0), axis=0, keepdims=True) > 0.0
        dests = [dest0, jnp.where(rose, 0.0, row1)]
        owned, places, groups = ranks(dests, my_row, 2 * NB)
        groups_ref[0] = groups

        factor10 = dot(n0_ref[...], upper_ref[0]).astype(bf16)
        u01_ref[...] = dot(lower_ref[0], n1_ref[...]).astype(bf16)

        for i in range(width // NB):
            at = slice(i * NB, (i + 1) * NB)
            u0 = dot(lower_ref[0], t_ref[:NB, at]).astype(bf16)
            t1 = (t_ref[NB:, at].astype(jnp.float32) - dot(factor10, u0)).astype(bf16)
            u1 = dot(lower_ref[1], t1).astype(bf16)
            if i == 0:
                special0, special1 = my_col == 0, my_col == 1
                top_ref[:NB, at] = jnp.where(special0, t_ref[:NB, at], u0)
                top_ref[NB:, at] = jnp.where(special0, factor10, jnp.where(special1, t1, u1))
                u0 = jnp.where(special0 | special1, jnp.zeros_like(u0), u0)
                u1 = jnp.where(special0 | special1, jnp.zeros_like(u1), u1)
            else:
                top_ref[:NB, at] = u0
                top_ref[NB:, at] = u1
            u_ref[:NB, at] = u0
            u_ref[NB:, at] = u1

        def one_group(group):
            at = pl.ds(pl.multiple_of(group * GROUP, GROUP), GROUP)
            hot = [choose(have, place, group) for have, place in zip(owned, places)]
            where_to = jnp.full((GROUP, 1), -1.0)
            for one, dest in zip(hot, dests):
                where_to = where_to + jnp.sum(one * (dest + 1.0), axis=1, keepdims=True)
            row_ref[pl.ds(pl.multiple_of(group * 8, 8), 8), :] = jnp.broadcast_to(flat(where_to), (8, GROUP))
            hot = [one.astype(bf16) for one in hot]

            def gather(ref, cols):
                return (dot(hot[0], ref[:NB, cols]) + dot(hot[1], ref[NB:, cols])).astype(bf16)

            f0, f1 = factors(gather(q_ref, slice(0, NB)), gather(q_ref, slice(NB, 2 * NB)))
            for c in range(width // NB):
                cols = slice(c * NB, (c + 1) * NB)
                w_ref[at, cols] = update(gather(o_ref, cols), f0, f1, c).astype(bf16)

        one_group(jnp.int32(0))

        @pl.loop(1, groups)
        def _(group):
            one_group(group)

    base = (step // 2 * 8 + my_row) * NB + step % 2 * 256
    held = base.astype(jnp.float32) + iota((rows, 1), 0)

    def landing(group):
        hot = jnp.where(held == row_ref[pl.ds(pl.multiple_of(group * 8, 8), 8), :][:1], 1.0, 0.0)
        return hot.astype(bf16), jnp.max(hot, axis=1, keepdims=True) > 0.0

    f0, f1 = factors(c0_ref[...], c1_ref[...])
    hot, moved = landing(jnp.int32(0))
    for c in range(width // NB):
        cols = slice(c * NB, (c + 1) * NB)
        fresh = update(tiles_ref[:, cols], f0, f1, c)
        out_ref[:, cols] = jnp.where(moved, dot(hot, w_ref[:GROUP, cols]), fresh).astype(bf16)

    @pl.loop(1, groups_ref[0])
    def _(group):
        hot, moved = landing(group)
        at = pl.ds(pl.multiple_of(group * GROUP, GROUP), GROUP)
        for c in range(width // NB):
            cols = slice(c * NB, (c + 1) * NB)
            kept = out_ref[:, cols].astype(jnp.float32)
            out_ref[:, cols] = jnp.where(moved, dot(hot, w_ref[at, cols]), kept).astype(bf16)

    for r in range(2):
        for part in range(2):
            @pl.when((my_row == r) & (step == part))
            def _():
                out_ref[...] = top_ref[r * NB + part * 256 : r * NB + (part + 1) * 256, :]


VMEM = pl.BlockSpec(memory_space=pltpu.VMEM)
SMEM = pl.BlockSpec(memory_space=pltpu.SMEM)
PARAMS = pltpu.CompilerParams(vmem_limit_bytes=58 << 20)


def body(matrix, pivots, lower_inverse, upper_inverse):
    row_blocks, block_width, col_blocks, _ = matrix.shape
    rows, width = row_blocks * block_width, col_blocks * block_width
    place = jnp.stack([lax.axis_index("prow"), lax.axis_index("pcol")]).astype(jnp.int32)
    tiles = matrix.reshape(rows, width)
    picked = pl.pallas_call(
        pick_kernel,
        out_shape=half(2 * NB, width),
        in_specs=[SMEM, VMEM, VMEM],
        out_specs=VMEM,
        scratch_shapes=[
            pltpu.VMEM((GROUP, rows), jnp.bfloat16),
            pltpu.VMEM((GROUP, 256), jnp.bfloat16),
            pltpu.VMEM((2 * NB, GROUP), jnp.bfloat16),
        ],
        compiler_params=PARAMS,
        name="pick",
    )(place, pivots, tiles)
    c0, c1, top_new, top_old, top_panels = exchange(tiles, picked)
    tile = pl.BlockSpec((256, width), lambda i: (i, 0))
    strip = pl.BlockSpec((256, NB), lambda i: (i, 0))
    rest = pl.BlockSpec((NB, NB), lambda i: (rows // NB, 0))
    out = pl.pallas_call(
        finish_kernel,
        grid=(rows // 256,),
        out_shape=half(rows, width),
        in_specs=[SMEM, VMEM, tile, strip, strip, rest, rest] + [VMEM] * 5,
        out_specs=tile,
        scratch_shapes=[pltpu.VMEM((2 * NB, width), jnp.bfloat16)] * 3
        + [pltpu.VMEM((NB, NB), jnp.bfloat16), pltpu.VMEM((8 * 2 * NB // GROUP, GROUP), jnp.float32),
           pltpu.SMEM((1,), jnp.int32)],
        compiler_params=pltpu.CompilerParams(vmem_limit_bytes=44 << 20),
        name="finish",
    )(place, pivots, tiles, c0, c1, c0, c1, top_new, top_old, top_panels, lower_inverse, upper_inverse)
    return out.reshape(matrix.shape)


def solution(mesh):
    placed = (P(None, "prow", None, "pcol"), P(), P(), P())
    return jax.shard_map(
        body, mesh=mesh, in_specs=placed, out_specs=P(None, "prow", None, "pcol"), check_vma=False
    )
```

```python
import functools

import jax
import jax.numpy as jnp
from jax import lax
from jax.experimental import pallas as pl
from jax.experimental.pallas import tpu as pltpu
from jax.sharding import PartitionSpec as P

MESH = pl.DeviceIdType.MESH
TREES = (
    1672, 6666386, 4867713, 2995995, 7311392, 13313154, 11448897, 5972163,
    9641992, 11515034, 9660058, 7845587, 11972616, 13845514, 12048003, 10176200,
    14303752, 16176264, 14378632, 12505288, 11915848, 13788296, 11990665, 10117848,
    9527880, 11400339, 9660058, 7730906, 7139916, 13198417, 7720961, 5859033,
)
NB = 512
PIECES = 2
HOP = 3
GAP = 5
EVERY = 1
CHAIN_AT = 20
SUM_AT = 1
SUM_GAP = 6
SUM_STEPS = (0, 1, 5, 6, 9, 10, 13, 16, 18)
SLOW_AT = 2
SLOW_GAP = 4
SLOW_STEPS = (0, 1, 5, 6, 10, 11, 15, 20, 24)
GROUP = 256


def exchange_kernel(
    tiles_ref, g_ref, c0_ref, c1_ref, t_ref, o_ref, q_ref,
    a_buf, h_buf, b1_buf, b2_buf,
    recv0, recv1, send0, send1, a_send, a_recv, b1_send, b1_recv, b2_send, b2_recv,
    d1_send, d1_recv, d2_send, d2_recv, e_send, e_recv,
    o_recv, o_next, o_side, o_other, q_recv, q_next, q_side, q_other, q_home,
):
    prow = lax.axis_index("prow")
    pcol = lax.axis_index("pcol")
    x, core = prow // 2, prow % 2
    z, y = pcol // 4, pcol % 4
    other = x * 2 + (1 - core)
    plane = [(z + 1) % 8 * 4 + y, (z + 7) % 8 * 4 + y, z * 4 + (y + 1) % 4, z * 4 + (y + 3) % 4]
    rows = 128 // PIECES
    blocks = tiles_ref.shape[0] // NB
    p = PIECES
    count = (blocks + 1) * p

    def lookup(place):
        code = jnp.int32(TREES[0])
        for i in range(1, 32):
            code = jnp.where(place == i, jnp.int32(TREES[i]), code)
        tree_of = [code // 8**i % 8 for i in range(4)]
        begin = [code // 8 ** (4 + i) % 8 * HOP for i in range(4)]
        wait_at = [jnp.where(place == 0, 1000, at) for at in begin]
        send_at = []
        for tree in tree_of:
            at = jnp.where(tree == 0, begin[0], 1000)
            for i in range(1, 4):
                at = jnp.where(tree == i, begin[i], at)
            send_at.append(at)
        return tree_of, begin, wait_at, send_at

    place = [pcol, z * 4 + (y + 3) % 4]
    trees = [lookup(place[0]), lookup(place[1])]
    panels = [c0_ref, c1_ref]
    recvs, sends = [recv0, recv1], [send0, send1]

    pair = [(x + 1 - 2 * (x % 2)) * 2 + core, (3 - x) * 2 + core]
    bit = [(x + 1) // 2 % 2, x // 2]
    ahead = [(x + 1) % 4 * 2 + core, (x + 3) % 4 * 2 + core]

    barrier = pltpu.get_barrier_semaphore()
    for d in range(4):
        pl.semaphore_signal(barrier, inc=1, device_id={"pcol": plane[d]}, device_id_type=MESH)
    for to in ahead + [other]:
        pl.semaphore_signal(barrier, inc=1, device_id={"prow": to}, device_id_type=MESH)
    pl.semaphore_wait(barrier, 7)

    def remote(src, dst, send, recv, **to):
        return pltpu.make_async_remote_copy(
            src_ref=src, dst_ref=dst, send_sem=send, recv_sem=recv, device_id=to, device_id_type=MESH
        )

    def arrival(ref, sem):
        return pltpu.make_async_copy(ref, ref, sem)

    def piece(t, j):
        start = j // p * NB + t * 128 + j % p * rows
        return pl.ds(pl.multiple_of(start, rows), rows)

    def tree_copy(r, t, j, d):
        at = panels[r].at[piece(t, j)]
        return remote(at, at, sends[r].at[d, j], recvs[r].at[t, j], pcol=plane[d])

    def slot(r, u):
        return (u >= 0) & (u < 2 * count) & (u % 2 == r), u // 2

    def tree_step(r, s):
        tree_of, begin, wait_at, send_at = trees[r]
        for t in range(4):
            due, j = slot(r, s - wait_at[t])

            @pl.when(due)
            def _():
                arrival(panels[r].at[piece(t, j)], recvs[r].at[t, j]).wait()

        for d in range(4):
            ready, i = slot(r, s - send_at[d])

            @pl.when(ready)
            def _():
                tree_copy(r, tree_of[d], i, d).start()

    def cols(h):
        return pl.ds(h * NB, NB)

    mine = pl.ds(pl.multiple_of(core * NB, NB), NB)
    theirs = pl.ds(pl.multiple_of((1 - core) * NB, NB), NB)

    def a_copy(h):
        return remote(g_ref.at[theirs, cols(h)], a_buf.at[h], a_send.at[h], a_recv.at[h], prow=other)

    def kept(e, sign):
        b = bit[e] if sign else 1 - bit[e]
        return pl.ds(pl.multiple_of(e * 256 + b * 128, 128), 128)

    def final(e, sign):
        b = bit[1 - e] if sign else 1 - bit[1 - e]
        return e * 256 + bit[e] * 128 + b * 64

    def b1_copy(h, e):
        return remote(h_buf.at[h, kept(e, False)], b1_buf.at[h, e], b1_send.at[h, e], b1_recv.at[h, e], prow=pair[e])

    def b2_copy(h, e):
        at = pl.ds(pl.multiple_of(final(e, False), 64), 64)
        return remote(h_buf.at[h, at], b2_buf.at[h, e], b2_send.at[h, e], b2_recv.at[h, e], prow=pair[1 - e])

    def d1_copy(h, e):
        ref = t_ref.at[pl.ds(pl.multiple_of(core * NB + final(e, True), 64), 64), cols(h)]
        return remote(ref, ref, d1_send.at[h, e], d1_recv.at[h, e], prow=pair[1 - e])

    def d2_copy(h, e):
        ref = t_ref.at[pl.ds(pl.multiple_of(core * NB + e * 256 + bit[e] * 128, 128), 128), cols(h)]
        return remote(ref, ref, d2_send.at[h, e], d2_recv.at[h, e], prow=pair[e])

    def e_copy(h):
        ref = t_ref.at[mine, cols(h)]
        return remote(ref, ref, e_send.at[h], e_recv.at[h], prow=other)

    def sum_step(h, k):
        if k == 0:
            a_copy(h).wait_recv()
            h_buf[h] = g_ref[mine, h * NB : (h + 1) * NB] + a_buf[h]
        elif k == 1:
            for e in range(2):
                b1_copy(h, e).start()
        elif k == 2:
            for e in range(2):
                b1_copy(h, e).wait_recv()
                h_buf[h, kept(e, True)] += b1_buf[h, e]
        elif k == 3:
            for e in range(2):
                b2_copy(h, e).start()
        elif k == 4:
            for e in range(2):
                b2_copy(h, e).wait_recv()
                at = final(e, True)
                t_ref[pl.ds(pl.multiple_of(core * NB + at, 64), 64), h * NB : (h + 1) * NB] = (
                    h_buf[h, pl.ds(pl.multiple_of(at, 64), 64)] + b2_buf[h, e]
                )
        elif k == 5:
            for e in range(2):
                d1_copy(h, e).start()
        elif k == 6:
            for e in range(2):
                d1_copy(h, e).wait_recv()
                d2_copy(h, e).start()
        elif k == 7:
            for e in range(2):
                d2_copy(h, e).wait_recv()
            e_copy(h).start()
        else:
            e_copy(h).wait_recv()

    far = [x, (4 - x) % 4]

    def link(h, c, of):
        return pl.ds(pl.multiple_of(of * NB + h * 256 + c * 64, 64), 64)

    def chain_send(ref, h, c, recv, forward):
        at = ref.at[link(h, c, core)]
        return remote(at, at, forward.at[h, c], recv.at[h, c], prow=ahead[h])

    def side_send(ref, h, c, side, opposite):
        at = ref.at[link(h, c, core)]
        return remote(at, at, side.at[h, c], opposite.at[h, c], prow=other)

    def chain_step(ref, h, c, recv, forward, side, opposite):
        arrival(ref.at[link(h, c, core)], recv.at[h, c]).wait()

        @pl.when(far[h] < 3)
        def _():
            chain_send(ref, h, c, recv, forward).start()

        side_send(ref, h, c, side, opposite).start()

    def home(h, c, i):
        at = pl.ds(h * 256 + c * 64, 64)
        return pltpu.make_async_copy(
            panels[i].at[at], q_ref.at[link(h, c, core), pl.ds(i * NB, NB)], q_home.at[h, c, i]
        )

    units = [(h, c) for h in range(2) for c in range(4)]

    for h in range(2):
        a_copy(h).start()

    @pl.when(x == 0)
    def _():
        for h, c in units:
            pltpu.make_async_copy(
                tiles_ref.at[pl.ds(h * 256 + c * 64, 64)], o_ref.at[link(h, c, core)], o_recv.at[h, c]
            ).start()

    for r in range(2):
        @pl.when(place[r] == 0)
        def _():
            own = pltpu.make_async_copy(
                tiles_ref.at[:, pl.ds(0, NB)], panels[r].at[pl.ds(0, blocks * NB)], a_send.at[2]
            )
            own.start()
            own.wait()

    top_at = 7 * HOP + 2 * p
    actions = {}

    def plan(step, action):
        actions.setdefault(step, []).append(action)

    def summing(h, k, hurry):
        @pl.when((pcol < 2) if hurry else (pcol >= 2))
        def _():
            sum_step(h, k)

    for h in range(2):
        for k, at in enumerate(SUM_STEPS):
            plan(SUM_AT + at + SUM_GAP * h, functools.partial(summing, h, k, True))
        for k, at in enumerate(SLOW_STEPS):
            plan(SLOW_AT + at + SLOW_GAP * h, functools.partial(summing, h, k, False))

    def root_rest():
        for r in range(2):
            @pl.when(place[r] == 0)
            def _():
                rest = pltpu.make_async_copy(
                    t_ref.at[pl.ds((1 - r) * NB, NB), pl.ds(0, NB)],
                    panels[r].at[pl.ds(blocks * NB, NB)], a_send.at[3],
                )
                rest.start()
                rest.wait()

    assert SUM_AT + SUM_STEPS[-1] < 2 * blocks * p
    plan(SUM_AT + SUM_STEPS[-1], root_rest)

    def old_rows(h, c, hop):
        @pl.when(far[h] == hop)
        def _():
            chain_step(o_ref, h, c, o_recv, o_next, o_side, o_other)

    def at_home():
        @pl.when(x == 0)
        def _():
            for h, c in units:
                for i in range(2):
                    home(h, c, i).start()

    def old_panels(h, c, hop):
        @pl.when(far[h] == hop)
        def _():
            if hop:
                chain_step(q_ref, h, c, q_recv, q_next, q_side, q_other)
            else:
                for i in range(2):
                    home(h, c, i).wait()
                chain_send(q_ref, h, c, q_recv, q_next).start()
                side_send(q_ref, h, c, q_side, q_other).start()

    for hop in range(4):
        for h, c in units:
            plan(CHAIN_AT + GAP * hop + EVERY * c, functools.partial(old_rows, h, c, hop))
            plan(top_at + 1 + GAP * hop + EVERY * c, functools.partial(old_panels, h, c, hop))
    plan(top_at, at_home)
    total = max(2 * count + 7 * HOP, max(actions) + 1)

    @pl.loop(0, total)
    def _(s):
        for r in range(2):
            tree_step(r, s)

        for first in range(0, total, 8):
            inside = [step for step in range(first, first + 8) if step in actions]
            if inside:
                @pl.when((s >= inside[0]) & (s <= inside[-1]))
                def _():
                    for step in inside:
                        @pl.when(s == step)
                        def _():
                            for action in actions[step]:
                                action()

    for r in range(2):
        tree_of = trees[r][0]

        @pl.loop(0, count)
        def _(j):
            for d in range(4):
                @pl.when(tree_of[d] < 4)
                def _():
                    tree_copy(r, 0, j, d).wait_send()

    for h in range(2):
        a_copy(h).wait_send()
        e_copy(h).wait_send()
        for e in range(2):
            for copy in (b1_copy, b2_copy, d1_copy, d2_copy):
                copy(h, e).wait_send()
    for ref, recv, forward, side, opposite in (
        (o_ref, o_recv, o_next, o_side, o_other), (q_ref, q_recv, q_next, q_side, q_other)
    ):
        for h, c in units:
            @pl.when(far[h] < 3)
            def _():
                chain_send(ref, h, c, recv, forward).wait_send()

            side_send(ref, h, c, side, opposite).wait_send()
            arrival(ref.at[link(h, c, 1 - core)], opposite.at[h, c]).wait()


def half(*shape):
    return jax.ShapeDtypeStruct(shape, jnp.bfloat16)


def exchange(tiles, picked):
    rows, width = tiles.shape
    vmem = pl.BlockSpec(memory_space=pltpu.VMEM)
    count = (rows // NB + 1) * PIECES
    dma = pltpu.SemaphoreType.DMA
    buf = functools.partial(pltpu.VMEM, dtype=jnp.bfloat16)
    return pl.pallas_call(
        exchange_kernel,
        out_shape=(half(rows + NB, NB), half(rows + NB, NB), half(2 * NB, width), half(2 * NB, width),
                   half(2 * NB, width)),
        in_specs=[pl.BlockSpec(memory_space=pl.ANY), vmem],
        out_specs=(vmem,) * 5,
        scratch_shapes=[buf((2, NB, NB)), buf((2, NB, NB)), buf((2, 2, 128, NB)), buf((2, 2, 64, NB)),
                        dma((4, count)), dma((4, count)), dma((4, count)), dma((4, count)),
                        dma((4,)), dma((2,))]
        + [dma((2, 2))] * 8 + [dma((2,))] * 2 + [dma((2, 4))] * 8 + [dma((2, 4, 2))],
        compiler_params=pltpu.CompilerParams(collective_id=0, has_side_effects=True, vmem_limit_bytes=24 << 20),
        name="exchange",
    )(tiles, picked)


def dot(a, b):
    return jnp.dot(a, b, preferred_element_type=jnp.float32)


def iota(shape, dim):
    return lax.broadcasted_iota(jnp.int32, shape, dim).astype(jnp.float32)


def upright(row):
    n = row.shape[1]
    return jnp.sum(jnp.where(iota((n, n), 0) == iota((n, n), 1), row, 0.0), axis=1, keepdims=True)


def flat(column):
    n = column.shape[0]
    return jnp.sum(jnp.where(iota((n, n), 0) == iota((n, n), 1), column, 0.0), axis=0, keepdims=True)


def pivot_vectors(piv_ref):
    rows = [piv_ref[i : i + 1, :].astype(jnp.float32) for i in range(2)]
    return rows, [upright(row) for row in rows]


def ranks(targets, my_row, least):
    before = jnp.where(iota((NB, NB), 0) < iota((NB, NB), 1), 1.0, 0.0).astype(jnp.bfloat16)
    owned, places, total = [], [], 0.0
    for target in targets:
        whole = target.astype(jnp.int32)
        held = jnp.where((whole // NB % 8 == my_row) & (whole >= least), 1.0, 0.0)
        ahead = dot(jnp.broadcast_to(held, (16, NB)).astype(jnp.bfloat16), before)[:1]
        owned.append(held > 0.0)
        places.append(ahead + total)
        total = total + jnp.sum(held)
    groups = (total.astype(jnp.int32) + GROUP - 1) // GROUP
    return owned, places, groups


def choose(owned, place, group):
    slot = iota((GROUP, 1), 0) + (group * GROUP).astype(jnp.float32)
    return jnp.where(owned & (place == slot), 1.0, 0.0)


def pick_kernel(place_ref, piv_ref, tiles_ref, g_ref, hot_ref, few_ref, many_ref):
    rows, width = tiles_ref.shape
    my_row = place_ref[0]
    (row0, row1), (col0, _) = pivot_vectors(piv_ref)
    same = col0 == row1
    index = jnp.sum(jnp.where(same, iota((NB, NB), 0), 0.0), axis=0, keepdims=True)
    found = jnp.max(jnp.where(same, 1.0, 0.0), axis=0, keepdims=True) > 0.0
    sources = [row0, jnp.where(found, index, row1)]
    owned, places, groups = ranks(sources, my_row, 0)
    tall = [upright(jnp.where(have, place, -1.0)) for have, place in zip(owned, places)]

    def one_group(group, first):
        wanted = jnp.full((GROUP, 1), -1.0)
        for source, have, place in zip(sources, owned, places):
            wanted = wanted + jnp.sum(choose(have, place, group) * (source + 1.0), axis=1, keepdims=True)
        for i in range(rows // NB):
            held = ((i * 8 + my_row) * NB).astype(jnp.float32) + iota((1, NB), 1)
            hot_ref[:, i * NB : (i + 1) * NB] = jnp.where(wanted == held, 1.0, 0.0).astype(jnp.bfloat16)
        slot = iota((1, GROUP), 1) + (group * GROUP).astype(jnp.float32)
        for i in range(2):
            many_ref[i * NB : (i + 1) * NB, :] = jnp.where(tall[i] == slot, 1.0, 0.0).astype(jnp.bfloat16)

        @pl.loop(0, width // 256)
        def _(i):
            at = pl.ds(pl.multiple_of(i * 256, 256), 256)
            few_ref[...] = dot(hot_ref[...], tiles_ref[:, at]).astype(jnp.bfloat16)
            spread = dot(many_ref[...], few_ref[...])
            if not first:
                spread = spread + g_ref[:, at].astype(jnp.float32)
            g_ref[:, at] = spread.astype(jnp.bfloat16)

    one_group(jnp.int32(0), True)

    @pl.loop(1, groups)
    def _(group):
        one_group(group, False)


def finish_kernel(
    place_ref, piv_ref, tiles_ref, c0_ref, c1_ref, n0_ref, n1_ref, t_ref, o_ref, q_ref, lower_ref, upper_ref,
    out_ref, u_ref, w_ref, top_ref, u01_ref, row_ref, groups_ref,
):
    my_row, my_col = place_ref[0], place_ref[1]
    step = pl.program_id(0)
    rows, width = tiles_ref.shape
    bf16 = jnp.bfloat16

    def factors(first, second):
        f0 = dot(first, upper_ref[0]).astype(bf16)
        rest = (second.astype(jnp.float32) - dot(f0, u01_ref[...])).astype(bf16)
        return f0, dot(rest, upper_ref[1]).astype(bf16)

    def update(old, f0, f1, c):
        at = slice(c * NB, (c + 1) * NB)
        if c == 0:
            old = jnp.where(my_col == 0, f0, jnp.where(my_col == 1, f1, old))
        old = (old.astype(jnp.float32) - dot(f0, u_ref[:NB, at])).astype(bf16)
        return old.astype(jnp.float32) - dot(f1, u_ref[NB:, at])

    @pl.when(step == 0)
    def _():
        (row0, row1), (col0, col1) = pivot_vectors(piv_ref)
        into = iota((NB, NB), 0) + NB == row0
        also = col1 == row0
        down = jnp.sum(jnp.where(into, col1, 0.0), axis=0, keepdims=True)
        back = jnp.sum(jnp.where(also, iota((NB, NB), 0) + NB, 0.0), axis=0, keepdims=True)
        went = jnp.max(jnp.where(into, 1.0, 0.0), axis=0, keepdims=True) > 0.0
        came = jnp.max(jnp.where(also, 1.0, 0.0), axis=0, keepdims=True) > 0.0
        dest0 = jnp.where(went, down, jnp.where(came, back, row0))
        up = col0 == iota((1, NB), 1) + NB
        rose = jnp.max(jnp.where(up, 1.0, 0.0), axis=0, keepdims=True) > 0.0
        dests = [dest0, jnp.where(rose, 0.0, row1)]
        owned, places, groups = ranks(dests, my_row, 2 * NB)
        groups_ref[0] = groups

        factor10 = dot(n0_ref[...], upper_ref[0]).astype(bf16)
        u01_ref[...] = dot(lower_ref[0], n1_ref[...]).astype(bf16)

        for i in range(width // NB):
            at = slice(i * NB, (i + 1) * NB)
            u0 = dot(lower_ref[0], t_ref[:NB, at]).astype(bf16)
            t1 = (t_ref[NB:, at].astype(jnp.float32) - dot(factor10, u0)).astype(bf16)
            u1 = dot(lower_ref[1], t1).astype(bf16)
            if i == 0:
                special0, special1 = my_col == 0, my_col == 1
                top_ref[:NB, at] = jnp.where(special0, t_ref[:NB, at], u0)
                top_ref[NB:, at] = jnp.where(special0, factor10, jnp.where(special1, t1, u1))
                u0 = jnp.where(special0 | special1, jnp.zeros_like(u0), u0)
                u1 = jnp.where(special0 | special1, jnp.zeros_like(u1), u1)
            else:
                top_ref[:NB, at] = u0
                top_ref[NB:, at] = u1
            u_ref[:NB, at] = u0
            u_ref[NB:, at] = u1

        def one_group(group):
            at = pl.ds(pl.multiple_of(group * GROUP, GROUP), GROUP)
            hot = [choose(have, place, group) for have, place in zip(owned, places)]
            where_to = jnp.full((GROUP, 1), -1.0)
            for one, dest in zip(hot, dests):
                where_to = where_to + jnp.sum(one * (dest + 1.0), axis=1, keepdims=True)
            row_ref[pl.ds(pl.multiple_of(group * 8, 8), 8), :] = jnp.broadcast_to(flat(where_to), (8, GROUP))
            hot = [one.astype(bf16) for one in hot]

            def gather(ref, cols):
                return (dot(hot[0], ref[:NB, cols]) + dot(hot[1], ref[NB:, cols])).astype(bf16)

            f0, f1 = factors(gather(q_ref, slice(0, NB)), gather(q_ref, slice(NB, 2 * NB)))
            for c in range(width // NB):
                cols = slice(c * NB, (c + 1) * NB)
                w_ref[at, cols] = update(gather(o_ref, cols), f0, f1, c).astype(bf16)

        one_group(jnp.int32(0))

        @pl.loop(1, groups)
        def _(group):
            one_group(group)

    base = (step // 2 * 8 + my_row) * NB + step % 2 * 256
    held = base.astype(jnp.float32) + iota((rows, 1), 0)

    def landing(group):
        hot = jnp.where(held == row_ref[pl.ds(pl.multiple_of(group * 8, 8), 8), :][:1], 1.0, 0.0)
        return hot.astype(bf16), jnp.max(hot, axis=1, keepdims=True) > 0.0

    f0, f1 = factors(c0_ref[...], c1_ref[...])
    hot, moved = landing(jnp.int32(0))
    for c in range(width // NB):
        cols = slice(c * NB, (c + 1) * NB)
        fresh = update(tiles_ref[:, cols], f0, f1, c)
        out_ref[:, cols] = jnp.where(moved, dot(hot, w_ref[:GROUP, cols]), fresh).astype(bf16)

    @pl.loop(1, groups_ref[0])
    def _(group):
        hot, moved = landing(group)
        at = pl.ds(pl.multiple_of(group * GROUP, GROUP), GROUP)
        for c in range(width // NB):
            cols = slice(c * NB, (c + 1) * NB)
            kept = out_ref[:, cols].astype(jnp.float32)
            out_ref[:, cols] = jnp.where(moved, dot(hot, w_ref[at, cols]), kept).astype(bf16)

    for r in range(2):
        for part in range(2):
            @pl.when((my_row == r) & (step == part))
            def _():
                out_ref[...] = top_ref[r * NB + part * 256 : r * NB + (part + 1) * 256, :]


VMEM = pl.BlockSpec(memory_space=pltpu.VMEM)
SMEM = pl.BlockSpec(memory_space=pltpu.SMEM)
PARAMS = pltpu.CompilerParams(vmem_limit_bytes=16 << 20)


def body(matrix, pivots, lower_inverse, upper_inverse):
    row_blocks, block_width, col_blocks, _ = matrix.shape
    rows, width = row_blocks * block_width, col_blocks * block_width
    place = jnp.stack([lax.axis_index("prow"), lax.axis_index("pcol")]).astype(jnp.int32)
    tiles = matrix.reshape(rows, width)
    picked = pl.pallas_call(
        pick_kernel,
        out_shape=half(2 * NB, width),
        in_specs=[SMEM, VMEM, VMEM],
        out_specs=VMEM,
        scratch_shapes=[
            pltpu.VMEM((GROUP, rows), jnp.bfloat16),
            pltpu.VMEM((GROUP, 256), jnp.bfloat16),
            pltpu.VMEM((2 * NB, GROUP), jnp.bfloat16),
        ],
        compiler_params=PARAMS,
        name="pick",
    )(place, pivots, tiles)
    c0, c1, top_new, top_old, top_panels = exchange(tiles, picked)
    tile = pl.BlockSpec((256, width), lambda i: (i, 0))
    strip = pl.BlockSpec((256, NB), lambda i: (i, 0))
    rest = pl.BlockSpec((NB, NB), lambda i: (rows // NB, 0))
    out = pl.pallas_call(
        finish_kernel,
        grid=(rows // 256,),
        out_shape=half(rows, width),
        in_specs=[SMEM, VMEM, tile, strip, strip, rest, rest] + [VMEM] * 5,
        out_specs=tile,
        scratch_shapes=[pltpu.VMEM((2 * NB, width), jnp.bfloat16)] * 3
        + [pltpu.VMEM((NB, NB), jnp.bfloat16), pltpu.VMEM((8 * 2 * NB // GROUP, GROUP), jnp.float32),
           pltpu.SMEM((1,), jnp.int32)],
        compiler_params=pltpu.CompilerParams(vmem_limit_bytes=24 << 20),
        name="finish",
    )(place, pivots, tiles, c0, c1, c0, c1, top_new, top_old, top_panels, lower_inverse, upper_inverse)
    return out.reshape(matrix.shape)


def solution(mesh):
    placed = (P(None, "prow", None, "pcol"), P(), P(), P())
    return jax.shard_map(
        body, mesh=mesh, in_specs=placed, out_specs=P(None, "prow", None, "pcol"), check_vma=False
    )
```

```python
import functools

import jax
import jax.numpy as jnp
from jax import lax
from jax.experimental import pallas as pl
from jax.experimental.pallas import tpu as pltpu
from jax.sharding import PartitionSpec as P

MESH = pl.DeviceIdType.MESH
TREES = (
    1672, 6666386, 4867713, 2995995, 7311392, 13313154, 11448897, 5972163,
    9641992, 11515034, 9660058, 7845587, 11972616, 13845514, 12048003, 10176200,
    14303752, 16176264, 14378632, 12505288, 11915848, 13788296, 11990665, 10117848,
    9527880, 11400339, 9660058, 7730906, 7139916, 13198417, 7720961, 5859033,
)
NB = 512
PIECES = 2
HOP = 3
GAP = 5
EVERY = 1
CHAIN_AT = 20
SUM_AT = 1
SUM_GAP = 6
SUM_STEPS = (0, 1, 5, 6, 9, 10, 13, 16, 18)
SLOW_AT = 2
SLOW_GAP = 4
SLOW_STEPS = (0, 1, 5, 6, 10, 11, 15, 20, 24)
GROUP = 256


def exchange_kernel(
    tiles_ref, g_ref, c0_ref, c1_ref, t_ref, o_ref, q_ref,
    a_buf, h_buf, b1_buf, b2_buf,
    recv0, recv1, send0, send1, a_send, a_recv, b1_send, b1_recv, b2_send, b2_recv,
    d1_send, d1_recv, d2_send, d2_recv, e_send, e_recv,
    o_recv, o_next, o_side, o_other, q_recv, q_next, q_side, q_other, q_home,
):
    prow = lax.axis_index("prow")
    pcol = lax.axis_index("pcol")
    x, core = prow // 2, prow % 2
    z, y = pcol // 4, pcol % 4
    other = x * 2 + (1 - core)
    plane = [(z + 1) % 8 * 4 + y, (z + 7) % 8 * 4 + y, z * 4 + (y + 1) % 4, z * 4 + (y + 3) % 4]
    rows = 128 // PIECES
    blocks = tiles_ref.shape[0] // NB
    p = PIECES
    count = (blocks + 1) * p

    def lookup(place):
        code = jnp.int32(TREES[0])
        for i in range(1, 32):
            code = jnp.where(place == i, jnp.int32(TREES[i]), code)
        tree_of = [code // 8**i % 8 for i in range(4)]
        begin = [code // 8 ** (4 + i) % 8 * HOP for i in range(4)]
        wait_at = [jnp.where(place == 0, 1000, at) for at in begin]
        send_at = []
        for tree in tree_of:
            at = jnp.where(tree == 0, begin[0], 1000)
            for i in range(1, 4):
                at = jnp.where(tree == i, begin[i], at)
            send_at.append(at)
        return tree_of, begin, wait_at, send_at

    place = [pcol, z * 4 + (y + 3) % 4]
    trees = [lookup(place[0]), lookup(place[1])]
    panels = [c0_ref, c1_ref]
    recvs, sends = [recv0, recv1], [send0, send1]

    pair = [(x + 1 - 2 * (x % 2)) * 2 + core, (3 - x) * 2 + core]
    bit = [(x + 1) // 2 % 2, x // 2]
    ahead = [(x + 1) % 4 * 2 + core, (x + 3) % 4 * 2 + core]

    barrier = pltpu.get_barrier_semaphore()
    for d in range(4):
        pl.semaphore_signal(barrier, inc=1, device_id={"pcol": plane[d]}, device_id_type=MESH)
    for to in ahead + [other]:
        pl.semaphore_signal(barrier, inc=1, device_id={"prow": to}, device_id_type=MESH)
    pl.semaphore_wait(barrier, 7)

    def remote(src, dst, send, recv, **to):
        return pltpu.make_async_remote_copy(
            src_ref=src, dst_ref=dst, send_sem=send, recv_sem=recv, device_id=to, device_id_type=MESH
        )

    def arrival(ref, sem):
        return pltpu.make_async_copy(ref, ref, sem)

    def piece(t, j):
        start = j // p * NB + t * 128 + j % p * rows
        return pl.ds(pl.multiple_of(start, rows), rows)

    def tree_copy(r, t, j, d):
        at = panels[r].at[piece(t, j)]
        return remote(at, at, sends[r].at[d, j], recvs[r].at[t, j], pcol=plane[d])

    def slot(r, u):
        return (u >= 0) & (u < 2 * count) & (u % 2 == r), u // 2

    def tree_step(r, s):
        tree_of, begin, wait_at, send_at = trees[r]
        for t in range(4):
            due, j = slot(r, s - wait_at[t])

            @pl.when(due)
            def _():
                arrival(panels[r].at[piece(t, j)], recvs[r].at[t, j]).wait()

        for d in range(4):
            ready, i = slot(r, s - send_at[d])

            @pl.when(ready)
            def _():
                tree_copy(r, tree_of[d], i, d).start()

    def cols(h):
        return pl.ds(h * NB, NB)

    mine = pl.ds(pl.multiple_of(core * NB, NB), NB)
    theirs = pl.ds(pl.multiple_of((1 - core) * NB, NB), NB)

    def a_copy(h):
        return remote(g_ref.at[theirs, cols(h)], a_buf.at[h], a_send.at[h], a_recv.at[h], prow=other)

    def kept(e, sign):
        b = bit[e] if sign else 1 - bit[e]
        return pl.ds(pl.multiple_of(e * 256 + b * 128, 128), 128)

    def final(e, sign):
        b = bit[1 - e] if sign else 1 - bit[1 - e]
        return e * 256 + bit[e] * 128 + b * 64

    def b1_copy(h, e):
        return remote(h_buf.at[h, kept(e, False)], b1_buf.at[h, e], b1_send.at[h, e], b1_recv.at[h, e], prow=pair[e])

    def b2_copy(h, e):
        at = pl.ds(pl.multiple_of(final(e, False), 64), 64)
        return remote(h_buf.at[h, at], b2_buf.at[h, e], b2_send.at[h, e], b2_recv.at[h, e], prow=pair[1 - e])

    def d1_copy(h, e):
        ref = t_ref.at[pl.ds(pl.multiple_of(core * NB + final(e, True), 64), 64), cols(h)]
        return remote(ref, ref, d1_send.at[h, e], d1_recv.at[h, e], prow=pair[1 - e])

    def d2_copy(h, e):
        ref = t_ref.at[pl.ds(pl.multiple_of(core * NB + e * 256 + bit[e] * 128, 128), 128), cols(h)]
        return remote(ref, ref, d2_send.at[h, e], d2_recv.at[h, e], prow=pair[e])

    def e_copy(h):
        ref = t_ref.at[mine, cols(h)]
        return remote(ref, ref, e_send.at[h], e_recv.at[h], prow=other)

    def sum_step(h, k):
        if k == 0:
            a_copy(h).wait_recv()
            h_buf[h] = g_ref[mine, h * NB : (h + 1) * NB] + a_buf[h]
        elif k == 1:
            for e in range(2):
                b1_copy(h, e).start()
        elif k == 2:
            for e in range(2):
                b1_copy(h, e).wait_recv()
                h_buf[h, kept(e, True)] += b1_buf[h, e]
        elif k == 3:
            for e in range(2):
                b2_copy(h, e).start()
        elif k == 4:
            for e in range(2):
                b2_copy(h, e).wait_recv()
                at = final(e, True)
                t_ref[pl.ds(pl.multiple_of(core * NB + at, 64), 64), h * NB : (h + 1) * NB] = (
                    h_buf[h, pl.ds(pl.multiple_of(at, 64), 64)] + b2_buf[h, e]
                )
        elif k == 5:
            for e in range(2):
                d1_copy(h, e).start()
        elif k == 6:
            for e in range(2):
                d1_copy(h, e).wait_recv()
                d2_copy(h, e).start()
        elif k == 7:
            for e in range(2):
                d2_copy(h, e).wait_recv()
            e_copy(h).start()
        else:
            e_copy(h).wait_recv()

    far = [x, (4 - x) % 4]

    def link(h, c, of):
        return pl.ds(pl.multiple_of(of * NB + h * 256 + c * 64, 64), 64)

    def chain_send(ref, h, c, recv, forward):
        at = ref.at[link(h, c, core)]
        return remote(at, at, forward.at[h, c], recv.at[h, c], prow=ahead[h])

    def side_send(ref, h, c, side, opposite):
        at = ref.at[link(h, c, core)]
        return remote(at, at, side.at[h, c], opposite.at[h, c], prow=other)

    def chain_step(ref, h, c, recv, forward, side, opposite):
        arrival(ref.at[link(h, c, core)], recv.at[h, c]).wait()

        @pl.when(far[h] < 3)
        def _():
            chain_send(ref, h, c, recv, forward).start()

        side_send(ref, h, c, side, opposite).start()

    def home(h, c, i):
        at = pl.ds(h * 256 + c * 64, 64)
        return pltpu.make_async_copy(
            panels[i].at[at], q_ref.at[link(h, c, core), pl.ds(i * NB, NB)], q_home.at[h, c, i]
        )

    units = [(h, c) for h in range(2) for c in range(4)]

    for h in range(2):
        a_copy(h).start()

    @pl.when(x == 0)
    def _():
        for h, c in units:
            pltpu.make_async_copy(
                tiles_ref.at[pl.ds(h * 256 + c * 64, 64)], o_ref.at[link(h, c, core)], o_recv.at[h, c]
            ).start()

    for r in range(2):
        @pl.when(place[r] == 0)
        def _():
            own = pltpu.make_async_copy(
                tiles_ref.at[:, pl.ds(0, NB)], panels[r].at[pl.ds(0, blocks * NB)], a_send.at[2]
            )
            own.start()
            own.wait()

    top_at = 7 * HOP + 2 * p
    actions = {}

    def plan(step, action):
        actions.setdefault(step, []).append(action)

    def summing(h, k, hurry):
        @pl.when((pcol < 2) if hurry else (pcol >= 2))
        def _():
            sum_step(h, k)

    for h in range(2):
        for k, at in enumerate(SUM_STEPS):
            plan(SUM_AT + at + SUM_GAP * h, functools.partial(summing, h, k, True))
        for k, at in enumerate(SLOW_STEPS):
            plan(SLOW_AT + at + SLOW_GAP * h, functools.partial(summing, h, k, False))

    def root_rest():
        for r in range(2):
            @pl.when(place[r] == 0)
            def _():
                rest = pltpu.make_async_copy(
                    t_ref.at[pl.ds((1 - r) * NB, NB), pl.ds(0, NB)],
                    panels[r].at[pl.ds(blocks * NB, NB)], a_send.at[3],
                )
                rest.start()
                rest.wait()

    assert SUM_AT + SUM_STEPS[-1] < 2 * blocks * p
    plan(SUM_AT + SUM_STEPS[-1], root_rest)

    def old_rows(h, c, hop):
        @pl.when(far[h] == hop)
        def _():
            chain_step(o_ref, h, c, o_recv, o_next, o_side, o_other)

    def at_home():
        @pl.when(x == 0)
        def _():
            for h, c in units:
                for i in range(2):
                    home(h, c, i).start()

    def old_panels(h, c, hop):
        @pl.when(far[h] == hop)
        def _():
            if hop:
                chain_step(q_ref, h, c, q_recv, q_next, q_side, q_other)
            else:
                for i in range(2):
                    home(h, c, i).wait()
                chain_send(q_ref, h, c, q_recv, q_next).start()
                side_send(q_ref, h, c, q_side, q_other).start()

    for hop in range(4):
        for h, c in units:
            plan(CHAIN_AT + GAP * hop + EVERY * c, functools.partial(old_rows, h, c, hop))
            plan(top_at + 1 + GAP * hop + EVERY * c, functools.partial(old_panels, h, c, hop))
    plan(top_at, at_home)
    total = max(2 * count + 7 * HOP, max(actions) + 1)

    @pl.loop(0, total)
    def _(s):
        for r in range(2):
            tree_step(r, s)

        for first in range(0, total, 8):
            inside = [step for step in range(first, first + 8) if step in actions]
            if inside:
                @pl.when((s >= inside[0]) & (s <= inside[-1]))
                def _():
                    for step in inside:
                        @pl.when(s == step)
                        def _():
                            for action in actions[step]:
                                action()

    for r in range(2):
        tree_of = trees[r][0]

        @pl.loop(0, count)
        def _(j):
            for d in range(4):
                @pl.when(tree_of[d] < 4)
                def _():
                    tree_copy(r, 0, j, d).wait_send()

    for h in range(2):
        a_copy(h).wait_send()
        e_copy(h).wait_send()
        for e in range(2):
            for copy in (b1_copy, b2_copy, d1_copy, d2_copy):
                copy(h, e).wait_send()
    for ref, recv, forward, side, opposite in (
        (o_ref, o_recv, o_next, o_side, o_other), (q_ref, q_recv, q_next, q_side, q_other)
    ):
        for h, c in units:
            @pl.when(far[h] < 3)
            def _():
                chain_send(ref, h, c, recv, forward).wait_send()

            side_send(ref, h, c, side, opposite).wait_send()
            arrival(ref.at[link(h, c, 1 - core)], opposite.at[h, c]).wait()


def half(*shape):
    return jax.ShapeDtypeStruct(shape, jnp.bfloat16)


def exchange(tiles, picked):
    rows, width = tiles.shape
    vmem = pl.BlockSpec(memory_space=pltpu.VMEM)
    count = (rows // NB + 1) * PIECES
    dma = pltpu.SemaphoreType.DMA
    buf = functools.partial(pltpu.VMEM, dtype=jnp.bfloat16)
    return pl.pallas_call(
        exchange_kernel,
        out_shape=(half(rows + NB, NB), half(rows + NB, NB), half(2 * NB, width), half(2 * NB, width),
                   half(2 * NB, width)),
        in_specs=[pl.BlockSpec(memory_space=pl.ANY), vmem],
        out_specs=(vmem,) * 5,
        scratch_shapes=[buf((2, NB, NB)), buf((2, NB, NB)), buf((2, 2, 128, NB)), buf((2, 2, 64, NB)),
                        dma((4, count)), dma((4, count)), dma((4, count)), dma((4, count)),
                        dma((4,)), dma((2,))]
        + [dma((2, 2))] * 8 + [dma((2,))] * 2 + [dma((2, 4))] * 8 + [dma((2, 4, 2))],
        compiler_params=pltpu.CompilerParams(collective_id=0, has_side_effects=True, vmem_limit_bytes=24 << 20),
        name="exchange",
    )(tiles, picked)


def dot(a, b):
    return jnp.dot(a, b, preferred_element_type=jnp.float32)


def iota(shape, dim):
    return lax.broadcasted_iota(jnp.int32, shape, dim).astype(jnp.float32)


def upright(row):
    n = row.shape[1]
    return jnp.sum(jnp.where(iota((n, n), 0) == iota((n, n), 1), row, 0.0), axis=1, keepdims=True)


def flat(column):
    n = column.shape[0]
    return jnp.sum(jnp.where(iota((n, n), 0) == iota((n, n), 1), column, 0.0), axis=0, keepdims=True)


def pivot_vectors(piv_ref):
    rows = [piv_ref[i : i + 1, :].astype(jnp.float32) for i in range(2)]
    return rows, [upright(row) for row in rows]


def ranks(targets, my_row, least):
    before = jnp.where(iota((NB, NB), 0) < iota((NB, NB), 1), 1.0, 0.0).astype(jnp.bfloat16)
    owned, places, total = [], [], 0.0
    for target in targets:
        whole = target.astype(jnp.int32)
        held = jnp.where((whole // NB % 8 == my_row) & (whole >= least), 1.0, 0.0)
        ahead = dot(jnp.broadcast_to(held, (16, NB)).astype(jnp.bfloat16), before)[:1]
        owned.append(held > 0.0)
        places.append(ahead + total)
        total = total + jnp.sum(held)
    groups = (total.astype(jnp.int32) + GROUP - 1) // GROUP
    return owned, places, groups


def choose(owned, place, group):
    slot = iota((GROUP, 1), 0) + (group * GROUP).astype(jnp.float32)
    return jnp.where(owned & (place == slot), 1.0, 0.0)


def pick_kernel(place_ref, piv_ref, tiles_ref, g_ref, hot_ref, few_ref, many_ref):
    rows, width = tiles_ref.shape
    my_row = place_ref[0]
    (row0, row1), (col0, _) = pivot_vectors(piv_ref)
    same = col0 == row1
    index = jnp.sum(jnp.where(same, iota((NB, NB), 0), 0.0), axis=0, keepdims=True)
    found = jnp.max(jnp.where(same, 1.0, 0.0), axis=0, keepdims=True) > 0.0
    sources = [row0, jnp.where(found, index, row1)]
    owned, places, groups = ranks(sources, my_row, 0)
    tall = [upright(jnp.where(have, place, -1.0)) for have, place in zip(owned, places)]

    def one_group(group, first):
        wanted = jnp.full((GROUP, 1), -1.0)
        for source, have, place in zip(sources, owned, places):
            wanted = wanted + jnp.sum(choose(have, place, group) * (source + 1.0), axis=1, keepdims=True)
        for i in range(rows // NB):
            held = ((i * 8 + my_row) * NB).astype(jnp.float32) + iota((1, NB), 1)
            hot_ref[:, i * NB : (i + 1) * NB] = jnp.where(wanted == held, 1.0, 0.0).astype(jnp.bfloat16)
        slot = iota((1, GROUP), 1) + (group * GROUP).astype(jnp.float32)
        for i in range(2):
            many_ref[i * NB : (i + 1) * NB, :] = jnp.where(tall[i] == slot, 1.0, 0.0).astype(jnp.bfloat16)

        @pl.loop(0, width // 256)
        def _(i):
            at = pl.ds(pl.multiple_of(i * 256, 256), 256)
            few_ref[...] = dot(hot_ref[...], tiles_ref[:, at]).astype(jnp.bfloat16)
            spread = dot(many_ref[...], few_ref[...])
            if not first:
                spread = spread + g_ref[:, at].astype(jnp.float32)
            g_ref[:, at] = spread.astype(jnp.bfloat16)

    one_group(jnp.int32(0), True)

    @pl.loop(1, groups)
    def _(group):
        one_group(group, False)


def finish_kernel(
    place_ref, piv_ref, tiles_ref, c0_ref, c1_ref, n0_ref, n1_ref, t_ref, o_ref, q_ref, lower_ref, upper_ref,
    out_ref, u_ref, w_ref, top_ref, u01_ref, row_ref, groups_ref,
):
    my_row, my_col = place_ref[0], place_ref[1]
    step = pl.program_id(0)
    rows, width = tiles_ref.shape
    bf16 = jnp.bfloat16

    def factors(first, second):
        f0 = dot(first, upper_ref[0]).astype(bf16)
        rest = (second.astype(jnp.float32) - dot(f0, u01_ref[...])).astype(bf16)
        return f0, dot(rest, upper_ref[1]).astype(bf16)

    def update(old, f0, f1, c):
        at = slice(c * NB, (c + 1) * NB)
        if c == 0:
            old = jnp.where(my_col == 0, f0, jnp.where(my_col == 1, f1, old))
        old = (old.astype(jnp.float32) - dot(f0, u_ref[:NB, at])).astype(bf16)
        return old.astype(jnp.float32) - dot(f1, u_ref[NB:, at])

    @pl.when(step == 0)
    def _():
        (row0, row1), (col0, col1) = pivot_vectors(piv_ref)
        into = iota((NB, NB), 0) + NB == row0
        also = col1 == row0
        down = jnp.sum(jnp.where(into, col1, 0.0), axis=0, keepdims=True)
        back = jnp.sum(jnp.where(also, iota((NB, NB), 0) + NB, 0.0), axis=0, keepdims=True)
        went = jnp.max(jnp.where(into, 1.0, 0.0), axis=0, keepdims=True) > 0.0
        came = jnp.max(jnp.where(also, 1.0, 0.0), axis=0, keepdims=True) > 0.0
        dest0 = jnp.where(went, down, jnp.where(came, back, row0))
        up = col0 == iota((1, NB), 1) + NB
        rose = jnp.max(jnp.where(up, 1.0, 0.0), axis=0, keepdims=True) > 0.0
        dests = [dest0, jnp.where(rose, 0.0, row1)]
        owned, places, groups = ranks(dests, my_row, 2 * NB)
        groups_ref[0] = groups

        factor10 = dot(n0_ref[...], upper_ref[0]).astype(bf16)
        u01_ref[...] = dot(lower_ref[0], n1_ref[...]).astype(bf16)

        for i in range(width // NB):
            at = slice(i * NB, (i + 1) * NB)
            u0 = dot(lower_ref[0], t_ref[:NB, at]).astype(bf16)
            t1 = (t_ref[NB:, at].astype(jnp.float32) - dot(factor10, u0)).astype(bf16)
            u1 = dot(lower_ref[1], t1).astype(bf16)
            if i == 0:
                special0, special1 = my_col == 0, my_col == 1
                top_ref[:NB, at] = jnp.where(special0, t_ref[:NB, at], u0)
                top_ref[NB:, at] = jnp.where(special0, factor10, jnp.where(special1, t1, u1))
                u0 = jnp.where(special0 | special1, jnp.zeros_like(u0), u0)
                u1 = jnp.where(special0 | special1, jnp.zeros_like(u1), u1)
            else:
                top_ref[:NB, at] = u0
                top_ref[NB:, at] = u1
            u_ref[:NB, at] = u0
            u_ref[NB:, at] = u1

        def one_group(group):
            at = pl.ds(pl.multiple_of(group * GROUP, GROUP), GROUP)
            hot = [choose(have, place, group) for have, place in zip(owned, places)]
            where_to = jnp.full((GROUP, 1), -1.0)
            for one, dest in zip(hot, dests):
                where_to = where_to + jnp.sum(one * (dest + 1.0), axis=1, keepdims=True)
            row_ref[pl.ds(pl.multiple_of(group * 8, 8), 8), :] = jnp.broadcast_to(flat(where_to), (8, GROUP))
            hot = [one.astype(bf16) for one in hot]

            def gather(ref, cols):
                return (dot(hot[0], ref[:NB, cols]) + dot(hot[1], ref[NB:, cols])).astype(bf16)

            f0, f1 = factors(gather(q_ref, slice(0, NB)), gather(q_ref, slice(NB, 2 * NB)))
            for c in range(width // NB):
                cols = slice(c * NB, (c + 1) * NB)
                w_ref[at, cols] = update(gather(o_ref, cols), f0, f1, c).astype(bf16)

        one_group(jnp.int32(0))

        @pl.loop(1, groups)
        def _(group):
            one_group(group)

    base = (step // 2 * 8 + my_row) * NB + step % 2 * 256
    held = base.astype(jnp.float32) + iota((rows, 1), 0)

    def landing(group):
        hot = jnp.where(held == row_ref[pl.ds(pl.multiple_of(group * 8, 8), 8), :][:1], 1.0, 0.0)
        return hot.astype(bf16), jnp.max(hot, axis=1, keepdims=True) > 0.0

    f0, f1 = factors(c0_ref[...], c1_ref[...])
    hot, moved = landing(jnp.int32(0))
    for c in range(width // NB):
        cols = slice(c * NB, (c + 1) * NB)
        fresh = update(tiles_ref[:, cols], f0, f1, c)
        out_ref[:, cols] = jnp.where(moved, dot(hot, w_ref[:GROUP, cols]), fresh).astype(bf16)

    @pl.loop(1, groups_ref[0])
    def _(group):
        hot, moved = landing(group)
        at = pl.ds(pl.multiple_of(group * GROUP, GROUP), GROUP)
        for c in range(width // NB):
            cols = slice(c * NB, (c + 1) * NB)
            kept = out_ref[:, cols].astype(jnp.float32)
            out_ref[:, cols] = jnp.where(moved, dot(hot, w_ref[at, cols]), kept).astype(bf16)

    for r in range(2):
        for part in range(2):
            @pl.when((my_row == r) & (step == part))
            def _():
                out_ref[...] = top_ref[r * NB + part * 256 : r * NB + (part + 1) * 256, :]


VMEM = pl.BlockSpec(memory_space=pltpu.VMEM)
SMEM = pl.BlockSpec(memory_space=pltpu.SMEM)
PARAMS = pltpu.CompilerParams(vmem_limit_bytes=16 << 20)


def body(matrix, pivots, lower_inverse, upper_inverse):
    row_blocks, block_width, col_blocks, _ = matrix.shape
    rows, width = row_blocks * block_width, col_blocks * block_width
    place = jnp.stack([lax.axis_index("prow"), lax.axis_index("pcol")]).astype(jnp.int32)
    tiles = matrix.reshape(rows, width)
    picked = pl.pallas_call(
        pick_kernel,
        out_shape=half(2 * NB, width),
        in_specs=[SMEM, VMEM, VMEM],
        out_specs=VMEM,
        scratch_shapes=[
            pltpu.VMEM((GROUP, rows), jnp.bfloat16),
            pltpu.VMEM((GROUP, 256), jnp.bfloat16),
            pltpu.VMEM((2 * NB, GROUP), jnp.bfloat16),
        ],
        compiler_params=PARAMS,
        name="pick",
    )(place, pivots, tiles)
    c0, c1, top_new, top_old, top_panels = exchange(tiles, picked)
    tile = pl.BlockSpec((256, width), lambda i: (i, 0))
    strip = pl.BlockSpec((256, NB), lambda i: (i, 0))
    rest = pl.BlockSpec((NB, NB), lambda i: (rows // NB, 0))
    out = pl.pallas_call(
        finish_kernel,
        grid=(rows // 256,),
        out_shape=pltpu.HBM((rows, width), jnp.bfloat16),
        in_specs=[SMEM, VMEM, tile, strip, strip, rest, rest] + [VMEM] * 5,
        out_specs=tile,
        scratch_shapes=[pltpu.VMEM((2 * NB, width), jnp.bfloat16)] * 3
        + [pltpu.VMEM((NB, NB), jnp.bfloat16), pltpu.VMEM((8 * 2 * NB // GROUP, GROUP), jnp.float32),
           pltpu.SMEM((1,), jnp.int32)],
        compiler_params=pltpu.CompilerParams(vmem_limit_bytes=24 << 20),
        name="finish",
    )(place, pivots, tiles, c0, c1, c0, c1, top_new, top_old, top_panels, lower_inverse, upper_inverse)
    return out.reshape(matrix.shape)


def solution(mesh):
    placed = (P(None, "prow", None, "pcol"), P(), P(), P())
    return jax.shard_map(
        body, mesh=mesh, in_specs=placed, out_specs=P(None, "prow", None, "pcol"), check_vma=False
    )
```
